256 devices in a mesh: tm: 16 (over x, y), ep: 16 (over z, core).
Axes of the slice: x: 4, y: 4, z: 8, core: 2. Of those that a mesh axis runs over, the one named last changes fastest.
Arguments:
- queries: bfloat16 [16, 2048, 2048], P('ep', 'tm'), may hold values from -6 to 6
- keys: bfloat16 [16, 2048, 2048], P('ep', 'tm'), may hold values from -6 to 6
- values: bfloat16 [16, 2048, 2048], P('ep', 'tm'), may hold values from -6 to 6
- residual_in: bfloat16 [16, 2048, 2048], P('ep', 'tm'), may hold values from -6 to 6
- attn_gain: float32 [2048], replicated, may hold values from 0.1 to 1.9
- out_proj: bfloat16 [2048, 2048], P('ep'), may hold values from -0.125 to 0.125
- ffn_gain: float32 [2048], replicated, may hold values from 0.1 to 1.9
- w_gate: bfloat16 [256, 2048, 256], P(('ep', 'tm')), may hold values from -0.125 to 0.125
- w_up: bfloat16 [256, 2048, 256], P(('ep', 'tm')), may hold values from -0.125 to 0.125
- w_down: bfloat16 [256, 256, 2048], P(('ep', 'tm')), may hold values from -0.1875 to 0.1875
- routes: int32 [16, 2048, 4], P('ep', 'tm'), may hold values from 0 to 63, all different within a row; in each aligned block of 32 rows (0 to 31, 32 to 63, ..., all dimensions but the last counted through in order) at most 4 rows name the same one
- gates: float32 [16, 2048, 4], P('ep', 'tm'), may hold values from 0.1 to 0.6
Outputs:
- layer_out: bfloat16 [16, 2048, 2048], P('ep', 'tm')
The draws below stay inside these ranges and needn't reach their ends.
Inputs may be any that keep to these rules, and one draw needn't show every extreme that they name: `routes`: each frame names 4 different experts. In each aligned block of 32 frames of a recording no expert is named by more than 4 frames, a bound that some block reaches.
All inputs are finite; a program needn't handle non-finite values.
Results may differ from the reference program's by a relative error of at most 0.007.
Values may be sent and summed in bfloat16 or wider, within the bound.
No kernel may reach another device: no remote copies, remote signals or barrier semaphores. Data moves between devices by JAX's collectives and lax.ppermute only.
A program may use at most 128 MiB of HBM per device.

```python
import math
from functools import partial
import jax
import jax.numpy as jnp
import numpy as np
from jax import lax

D = 2048
HEADS = 16
DH = 128
FF = 1024
TOPK = 4
T_DEV = 128
EXPERTS = 64
GROUPS = 4
BLK = 32
MOST = 4
REC = 16
TIME = 2048
N_TM = 16


def shard_levels(rng, shape, shards, low, largest):
    level = 1.0
    for dim, shards_of in shards:
        heights = jax.random.uniform(jax.random.fold_in(jax.random.fold_in(rng, 6), dim), (shards_of,), jnp.float32, low / len(shards), largest / len(shards))
        level = level * jnp.repeat(jnp.exp(heights), shape[dim] // shards_of).reshape((-1,) + (1,) * (len(shape) - 1 - dim))
    return level


def routed_block(rng, own, number, rows, number_of, top, most, lean):
    ranking = jax.random.permutation(rng, number_of)
    crowded, common = load_shares(number_of, rows * top, most, lean, True), load_shares(number_of, rows * top, most, lean, False)
    places = jnp.arange(number_of)

    def named(sizes, turn):
        used = int((sizes > 0).sum())
        fixed = max(1, used // 4)
        passed = fixed + (places - fixed + turn * (used - fixed)) % max(1, number_of - fixed)
        return jnp.zeros((number_of,), jnp.int32).at[ranking[jnp.where(places < fixed, places, passed)]].set(jnp.asarray(sizes, jnp.int32))

    sizes = jnp.where(number % 4 == 0, named(crowded, number // 4), named(common, number - number // 4 - 1))
    mixed = jax.random.permutation(jax.random.fold_in(own, 3), number_of)
    source_of, taker = mixed[0:number_of // 2 * 2:2], mixed[1:number_of // 2 * 2:2]
    margin = jnp.minimum(sizes[source_of] - 1, most - sizes[taker]) // 2
    margin = jnp.where((source_of == ranking[0]) | (taker == ranking[0]) | (sizes[taker] == 0), 0, jnp.maximum(margin, 0))
    passed = jax.random.randint(jax.random.fold_in(own, 4), (number_of // 2,), 0, 1 << 20) % (margin + 1)
    sizes = sizes.at[source_of].add(-passed).at[taker].add(passed)
    labels = jnp.searchsorted(jnp.cumsum(sizes), jnp.arange(rows * top), side="right").astype(jnp.int32)
    table = labels.reshape(top, rows).T
    table = table[jax.random.permutation(jax.random.fold_in(own, 1), rows)]
    turn = jax.random.randint(jax.random.fold_in(own, 2), (rows, 1), 0, top)
    return jnp.take_along_axis(table, (jnp.arange(top)[None, :] + turn) % top, axis=1)


def load_shares(number_of, total, limit, lean, full):
    portions = [(1 << 20) // math.isqrt(rank ** lean) + 1 for rank in range(1, number_of + 1)]
    largest = limit if full else min(limit, max(-(-total // number_of), total * portions[0] // sum(portions)))
    least = 1 if total - largest >= number_of - 1 else 0
    holding, spare = [largest] + [least] * (number_of - 1), total - largest - least * (number_of - 1)
    while spare > 0:
        free = [i for i in range(1, number_of) if holding[i] < largest] or [i for i in range(1, number_of) if holding[i] < limit]
        whole, left = sum([portions[i] for i in free]), spare
        for i in free:
            more = min(limit - holding[i], max(1, left * portions[i] // whole), spare)
            holding[i] = holding[i] + more
            spare = spare - more
    return np.array(holding)


def noise(stream_key, extent, deviation, limit, pieces=(), held_as=jnp.bfloat16):
    gain = shard_levels(stream_key, extent, pieces, -0.22, 0.18) if pieces else 1.0
    values = jax.random.normal(stream_key, extent, jnp.float32) * deviation * gain
    return jnp.minimum(jnp.maximum(values, -limit), limit).astype(held_as)


def setup_inputs(seed: int = 0) -> dict:
    streams_of = jax.random.split(jax.random.key(seed), 13)
    queries = noise(streams_of[0], (REC, TIME, D), 1.0, 6.0, ((0, 16), (1, 16)))
    keys = noise(streams_of[1], (REC, TIME, D), 1.0, 6.0, ((0, 16), (1, 16)))
    values = noise(streams_of[2], (REC, TIME, D), 1.0, 6.0, ((0, 16), (1, 16)))
    residual_in = noise(streams_of[3], (REC, TIME, D), 1.0, 6.0, ((0, 16), (1, 16)))
    attn_gain = jnp.clip(1.0 + 0.18 * jax.random.normal(streams_of[4], (D,), jnp.float32), 0.1, 1.9)
    out_proj = noise(streams_of[5], (D, D), D ** -0.5, 0.125, ((0, 16),))
    ffn_gain = jnp.clip(1.0 + 0.18 * jax.random.normal(streams_of[6], (D,), jnp.float32), 0.1, 1.9)
    w_gate = noise(streams_of[7], (EXPERTS * GROUPS, D, FF // GROUPS), D ** -0.5, 0.125, ((0, 256),))
    w_up = noise(streams_of[8], (EXPERTS * GROUPS, D, FF // GROUPS), D ** -0.5, 0.125, ((0, 256),))
    w_down = noise(streams_of[9], (EXPERTS * GROUPS, FF // GROUPS, D), FF ** -0.5, 0.1875, ((0, 256),))
    routes_keys = jax.random.split(jax.random.fold_in(streams_of[10], 1), REC * TIME // BLK)
    routes_turns = jax.random.permutation(jax.random.fold_in(streams_of[10], 3), REC * TIME // BLK)
    routes = jax.vmap(lambda own, number: routed_block(jax.random.fold_in(streams_of[10], 2), own, number, BLK, EXPERTS, TOPK, MOST, 2))(routes_keys, routes_turns).reshape((REC, TIME, TOPK))
    gates = jnp.clip(0.1 + 0.5 * jax.random.uniform(streams_of[11], (REC, TIME, TOPK), jnp.float32) ** shard_levels(streams_of[11], (REC, TIME, TOPK), ((0, 16), (1, 16)), -0.2, 0.2), 0.1, 0.6)
    return {"queries": queries, "keys": keys, "values": values, "residual_in": residual_in, "attn_gain": attn_gain, "out_proj": out_proj, "ffn_gain": ffn_gain, "w_gate": w_gate, "w_up": w_up, "w_down": w_down, "routes": routes, "gates": gates}


EPS = 1e-05
HIGH = lax.Precision.HIGHEST

def attend_recording(attn_gain, triple):
    query_in, key_in, value_in = triple
    block_shape = (N_TM, T_DEV, HEADS, DH)
    query_full = query_in.reshape(block_shape).astype(jnp.float32)
    key_full = key_in.reshape(block_shape).astype(jnp.float32)
    value_full = value_in.reshape(block_shape).astype(jnp.float32)
    scores = jnp.einsum('cthd,cshd->chts', query_full, key_full, precision=HIGH)
    causal = jnp.arange(T_DEV, dtype=jnp.int32)[:, None] >= jnp.arange(T_DEV, dtype=jnp.int32)[None, :]
    block_scores = jnp.where(causal, scores, 0.0).astype(jnp.bfloat16)
    local_part = jnp.einsum('chts,cshd->cthd', block_scores.astype(jnp.float32), value_full, precision=HIGH)
    block_state = jnp.einsum('cthd,cthe->chde', key_full, value_full, precision=HIGH)
    running = jnp.cumsum(block_state, axis=0)
    prefix = jnp.concatenate([jnp.zeros_like(block_state[:1]), running[:-1]], axis=0)
    prefix_low = prefix.astype(jnp.bfloat16)
    mixed = local_part + jnp.einsum('cthd,chde->cthe', query_full, prefix_low.astype(jnp.float32), precision=HIGH)
    head_scale = lax.rsqrt(lax.optimization_barrier(jnp.mean(mixed * mixed, axis=-1, keepdims=True)) + EPS)
    attended = mixed * head_scale * attn_gain.reshape(HEADS, DH)
    return attended.reshape(TIME, HEADS * DH).astype(jnp.bfloat16)

def reference(queries, keys, values, residual_in, attn_gain, out_proj, ffn_gain, w_gate, w_up, w_down, routes, gates):
    attended = lax.map(partial(attend_recording, attn_gain), (queries, keys, values))
    count_all = REC * TIME
    attended_flat = attended.reshape(count_all, D)
    projected = jnp.dot(attended_flat, out_proj, preferred_element_type=jnp.float32)
    residual_sum = residual_in.reshape(count_all, D).astype(jnp.float32) + projected
    norm_scale = lax.rsqrt(lax.optimization_barrier(jnp.mean(residual_sum * residual_sum, axis=-1, keepdims=True)) + EPS)
    normed = (residual_sum * norm_scale * ffn_gain).astype(jnp.bfloat16)
    normed_pad = jnp.concatenate([normed, jnp.zeros((1, D), jnp.bfloat16)], axis=0)
    choice_flat = routes.reshape(-1).astype(jnp.int32)
    route_count = count_all * TOPK
    order = jnp.argsort(choice_flat, stable=True).astype(jnp.int32)
    counts = lax.optimization_barrier(jnp.sum((choice_flat[:, None] == jnp.arange(EXPERTS, dtype=jnp.int32)[None, :]).astype(jnp.int32), axis=0))
    offsets = (jnp.cumsum(counts) - counts).astype(jnp.int32)
    block_rows = 512
    order_pad = jnp.concatenate([order, jnp.full((block_rows,), route_count, jnp.int32)])
    gate_pad = jnp.concatenate([gates.reshape(-1).astype(jnp.float32), jnp.zeros((1,), jnp.float32)])

    def expert_step(expert, mixture):
        first_row = offsets[expert]
        total_rows = counts[expert]
        base = (expert * GROUPS).astype(jnp.int32)
        gate_whole = lax.dynamic_slice_in_dim(w_gate, base, GROUPS, 0).transpose(1, 0, 2).reshape(D, FF)
        up_whole = lax.dynamic_slice_in_dim(w_up, base, GROUPS, 0).transpose(1, 0, 2).reshape(D, FF)
        down_whole = lax.dynamic_slice_in_dim(w_down, base, GROUPS, 0).reshape(FF, D)

        def block_step(index, inner):
            local_rows = jnp.arange(block_rows, dtype=jnp.int32) + index * block_rows
            route_ids = lax.dynamic_slice_in_dim(order_pad, (first_row + index * block_rows).astype(jnp.int32), block_rows)
            route_ids = jnp.where(local_rows < total_rows, route_ids, route_count)
            token_ids = route_ids // TOPK
            rows_in = normed_pad[token_ids]
            gate_act = jnp.dot(rows_in, gate_whole, preferred_element_type=jnp.float32)
            up_act = jnp.dot(rows_in, up_whole, preferred_element_type=jnp.float32)
            hidden = (jax.nn.silu(gate_act) * up_act).astype(jnp.bfloat16)
            expert_out = jnp.dot(hidden, down_whole, preferred_element_type=jnp.float32).astype(jnp.bfloat16)
            weight_rows = gate_pad[route_ids]
            return inner.at[token_ids].add(weight_rows[:, None] * expert_out.astype(jnp.float32), mode='drop')
        steps_needed = (total_rows + block_rows - 1) // block_rows
        return lax.fori_loop(0, steps_needed, block_step, mixture)
    mixture = lax.fori_loop(0, EXPERTS, expert_step, jnp.zeros((count_all, D), jnp.float32))
    layer_out = (residual_sum + mixture).astype(jnp.bfloat16)
    return layer_out.reshape(REC, TIME, D)
```

```python
import jax
import jax.numpy as jnp
from jax import lax
from jax.experimental import pallas as pl
from jax.experimental.pallas import tpu as pltpu
from jax.sharding import Mesh
from jax.sharding import PartitionSpec as P

HEADS = 16
DH = 128
D = 2048
T = 128
BLK = 32
MOST = 4
NX = 4
NZ = 8
SLOTS = T // BLK * MOST
HID = 256
EPS = 1e-05
MIB = 1 << 20
BF = jnp.bfloat16
F32 = jnp.float32


def dot(a, b, ca=1, cb=0):
    return lax.dot_general(a, b, (((ca,), (cb,)), ((), ())), preferred_element_type=F32)


def shift(value, axis, step):
    count = lax.axis_size(axis)
    return lax.ppermute(value, axis, [(i, (i + step) % count) for i in range(count)])


def head_block():
    return pl.BlockSpec((T, DH), lambda h: (0, h))


def state_kernel(k_ref, v_ref, state_ref):
    state_ref[0] = dot(k_ref[...], v_ref[...], 0, 0)


def block_states(keys, values):
    return pl.pallas_call(
        state_kernel,
        grid=(HEADS,),
        in_specs=[head_block(), head_block()],
        out_specs=pl.BlockSpec((1, DH, DH), lambda h: (h, 0, 0)),
        out_shape=jax.ShapeDtypeStruct((HEADS, DH, DH), F32),
        name="block_states",
    )(keys, values)


def local_kernel(q_ref, k_ref, v_ref, out_ref):
    scores = dot(q_ref[...], k_ref[...], 1, 1)
    rows = lax.broadcasted_iota(jnp.int32, (T, T), 0)
    columns = lax.broadcasted_iota(jnp.int32, (T, T), 1)
    scores = jnp.where(rows >= columns, scores, 0.0).astype(BF)
    out_ref[...] = dot(scores, v_ref[...])


def local_parts(queries, keys, values):
    return pl.pallas_call(
        local_kernel,
        grid=(HEADS,),
        in_specs=[head_block(), head_block(), head_block()],
        out_specs=head_block(),
        out_shape=jax.ShapeDtypeStruct((T, D), F32),
        name="local_parts",
    )(queries, keys, values)


def project_kernel(
    q_ref, local_ref, prefix_ref, gain_ref, w_ref, res_ref, fgain_ref, sum_ref, normed_ref, acc
):
    head = pl.program_id(0)
    mixed = local_ref[...] + dot(q_ref[...], prefix_ref[0])
    scale = lax.rsqrt(jnp.mean(mixed * mixed, axis=-1, keepdims=True) + EPS)
    attended = (mixed * scale * gain_ref[...]).astype(BF)
    part = dot(attended, w_ref[...])

    @pl.when(head == 0)
    def _():
        acc[...] = res_ref[...].astype(F32) + part

    @pl.when(head > 0)
    def _():
        acc[...] += part

    @pl.when(head == HEADS - 1)
    def _():
        total = acc[...]
        norm = lax.rsqrt(jnp.mean(total * total, axis=-1, keepdims=True) + EPS)
        sum_ref[...] = total
        normed_ref[...] = (total * norm * fgain_ref[...]).astype(BF)


def project(queries, local, prefix_low, attn_gain, weight, residual, ffn_gain):
    whole = pl.BlockSpec((T, D), lambda h: (0, 0))
    return pl.pallas_call(
        project_kernel,
        grid=(HEADS,),
        in_specs=[
            head_block(),
            head_block(),
            pl.BlockSpec((1, DH, DH), lambda h: (h, 0, 0)),
            pl.BlockSpec((1, DH), lambda h: (0, h)),
            pl.BlockSpec((DH, D), lambda h: (h, 0)),
            whole,
            pl.BlockSpec((1, D), lambda h: (0, 0)),
        ],
        out_specs=[whole, whole],
        out_shape=[jax.ShapeDtypeStruct((T, D), F32), jax.ShapeDtypeStruct((T, D), BF)],
        scratch_shapes=[pltpu.VMEM((T, D), F32)],
        name="project",
    )(queries, local, prefix_low, attn_gain, weight, residual, ffn_gain)


def exclusive_prefix(states):
    running = jnp.zeros_like(states[0])
    out = []
    for i in range(states.shape[0]):
        out.append(running.astype(BF))
        running = running + states[i]
    return jnp.stack(out)


def route_tables(routes, gates, x, z, c):
    meta = jnp.concatenate([routes[0].T.astype(F32), gates[0].T], axis=0)
    meta = jnp.stack([meta, shift(meta, "c", 1)])[None]
    for step in (1, 2, 4):
        meta = jnp.concatenate([meta, shift(meta, "z", -step)], axis=0)
    meta = meta.reshape(2 * NZ, 8, T)
    picks, gains = meta[:, :MOST], meta[:, MOST:]
    offsets = jnp.arange(NX, dtype=jnp.int32)
    experts = ((2 * z + c) * NX + (x + offsets) % NX).astype(F32)
    hit = picks[:, None, :, :] == experts[None, :, None, None]
    named = jnp.any(hit, axis=2)
    gain = jnp.sum(jnp.where(hit, gains[:, None], 0.0), axis=2)
    frame = jnp.arange(T, dtype=jnp.int32)
    earlier = (frame[:, None] < frame[None, :]) & (frame[:, None] // BLK == frame[None, :] // BLK)
    rank = lax.dot_general(
        named.astype(BF), earlier.astype(BF), (((2,), (0,)), ((), ())), preferred_element_type=F32
    )
    slot = rank.astype(jnp.int32) + frame // BLK * MOST
    taken = named & (rank < MOST)
    match = taken[:, :, None, :] & (
        slot[:, :, None, :] == jnp.arange(SLOTS, dtype=jnp.int32)[None, None, :, None]
    )
    select = match.astype(BF).reshape(2 * NZ, NX * SLOTS, T)
    high = lax.reduce_precision(gain, 8, 7)
    low = gain - high
    split = [
        jnp.where(match, part[:, :, None, :], 0.0).astype(BF).reshape(2 * NZ, NX * SLOTS, T)
        for part in (high, low)
    ]
    return select, jnp.concatenate(split, axis=1)


TILE = 512


def pick_kernel(count, s_ref, *refs):
    blocks, (a0, p1, p2, m2, m3) = refs[:count], refs[count:]
    half = count // 2
    for i in range(count):
        rows = dot(s_ref[i], blocks[i][...]).astype(BF)
        at = pl.ds(i * SLOTS, SLOTS)
        a0[at, :] = rows[:SLOTS]
        p1[at, :] = rows[SLOTS : 2 * SLOTS]
        mid = p2 if i < half else m2
        mid[pl.ds(i % half * SLOTS, SLOTS), :] = rows[2 * SLOTS : 3 * SLOTS]
        m3[at, :] = rows[3 * SLOTS :]


def row_counts(count):
    full, half = count * SLOTS, count // 2 * SLOTS
    return (full, full, half, half, full)


def column_tile(rows):
    return pl.BlockSpec((rows, TILE), lambda j: (0, j))


def pick_rows(select, blocks):
    count = len(blocks)
    sizes = row_counts(count)
    return pl.pallas_call(
        lambda *refs: pick_kernel(count, *refs),
        grid=(D // TILE,),
        in_specs=[pl.BlockSpec((count, NX * SLOTS, T), lambda j: (0, 0, 0))]
        + [column_tile(T)] * count,
        out_specs=[column_tile(n) for n in sizes],
        out_shape=[jax.ShapeDtypeStruct((n, D), BF) for n in sizes],
        compiler_params=pltpu.CompilerParams(vmem_limit_bytes=40 * MIB),
        name="pick_rows",
    )(select, *blocks)


def mix_kernel(count, t_ref, a0, p1, p2, m2, m3, *outs):
    half = count // 2
    for i in range(count):
        at = pl.ds(i * SLOTS, SLOTS)
        mid = p2 if i < half else m2
        rows = jnp.concatenate(
            [a0[at, :], p1[at, :], mid[pl.ds(i % half * SLOTS, SLOTS), :], m3[at, :]], axis=0
        )
        rows = jnp.concatenate([rows, rows], axis=0)
        outs[i % 2][pl.ds(i // 2 * T, T), :] = dot(t_ref[i], rows, 0, 0).astype(BF)


def mix_rows(weights, buffers):
    count = weights.shape[0]
    rows = count // 2 * T
    return pl.pallas_call(
        lambda *refs: mix_kernel(count, *refs),
        grid=(D // TILE,),
        in_specs=[pl.BlockSpec((count, 2 * NX * SLOTS, T), lambda j: (0, 0, 0))]
        + [column_tile(n) for n in row_counts(count)],
        out_specs=[column_tile(rows)] * 2,
        out_shape=[jax.ShapeDtypeStruct((rows, D), BF)] * 2,
        compiler_params=pltpu.CompilerParams(vmem_limit_bytes=40 * MIB),
        name="mix_rows",
    )(weights, *buffers)


def expert_kernel(sizes, *refs):
    n_in = len(sizes)
    inputs, weights = refs[:n_in], refs[n_in : n_in + 15]
    outs = refs[n_in + 15 : n_in + 15 + n_in]
    x_buf, g_buf, u_buf, d_buf, h_buf, x_sem, g_sem, u_sem, d_sem = refs[n_in + 15 + n_in :]
    starts = [sum(sizes[:i]) for i in range(n_in)]
    rows = sum(sizes)
    x_copies = [
        pltpu.make_async_copy(inputs[i], x_buf.at[pl.ds(starts[i], sizes[i])], x_sem.at[i])
        for i in range(n_in)
    ]
    half = D // 2
    targets = [(0, 0, D), (1, 0, D), (2, 0, D), (3, 0, half), (3, half, half)]

    def up_copies(kind, buf, sem):
        return [
            pltpu.make_async_copy(
                weights[kind * 5 + i], buf.at[g, pl.ds(first, size)], sem.at[i]
            )
            for i, (g, first, size) in enumerate(targets)
        ]

    g_copies, u_copies = up_copies(0, g_buf, g_sem), up_copies(1, u_buf, u_sem)
    d_places = [(0, HID), (HID, HID), (2 * HID, HID), (3 * HID, HID // 2), (7 * HID // 2, HID // 2)]
    d_copies = [
        pltpu.make_async_copy(weights[10 + i], d_buf.at[pl.ds(first, size)], d_sem.at[i])
        for i, (first, size) in enumerate(d_places)
    ]
    for copy in x_copies:
        copy.start()
    for i in range(5):
        g_copies[i].start()
        u_copies[i].start()
    for copy in d_copies:
        copy.start()
    for copy in x_copies:
        copy.wait()
    step = 256
    for g in range(4):
        for i in ([g], [3, 4])[g == 3]:
            g_copies[i].wait()
            u_copies[i].wait()

        def hidden_rows(r, _):
            at = pl.ds(pl.multiple_of(r * step, step), step)
            gate = dot(x_buf[at, :], g_buf[g])
            up = dot(x_buf[at, :], u_buf[g])
            h_buf[at, pl.ds(g * HID, HID)] = (gate / (1.0 + jnp.exp(-gate)) * up).astype(BF)
            return 0

        lax.fori_loop(0, rows // step, hidden_rows, 0)
    for copy in d_copies:
        copy.wait()
    for i in range(n_in):
        for first in range(0, sizes[i], 128):
            outs[i][pl.ds(first, 128), :] = dot(
                h_buf[pl.ds(starts[i] + first, 128), :], d_buf[...]
            ).astype(BF)


def experts_apply(buffers, weights):
    sizes = tuple(b.shape[0] for b in buffers)
    rows = sum(sizes)
    anywhere = pl.BlockSpec(memory_space=pl.ANY)
    return pl.pallas_call(
        lambda *refs: expert_kernel(sizes, *refs),
        in_specs=[anywhere] * (len(sizes) + 15),
        out_specs=[pl.BlockSpec(memory_space=pltpu.VMEM)] * len(sizes),
        out_shape=[jax.ShapeDtypeStruct((n, D), BF) for n in sizes],
        scratch_shapes=[
            pltpu.VMEM((rows, D), BF),
            pltpu.VMEM((4, D, HID), BF),
            pltpu.VMEM((4, D, HID), BF),
            pltpu.VMEM((4 * HID, D), BF),
            pltpu.VMEM((rows, 4 * HID), BF),
            pltpu.SemaphoreType.DMA((len(sizes),)),
            pltpu.SemaphoreType.DMA((5,)),
            pltpu.SemaphoreType.DMA((5,)),
            pltpu.SemaphoreType.DMA((5,)),
        ],
        compiler_params=pltpu.CompilerParams(vmem_limit_bytes=48 * MIB),
        name="experts",
    )(*buffers, *weights)


def join_pieces(piece):
    half = piece.shape[0] // 2
    below, above = shift(piece, "y", 1), shift(piece, "y", -1)
    far_first = shift(below[:half], "y", 1)
    far_second = shift(above[half:], "y", -1)
    return [piece, below, above, far_first, far_second]


def gather_z(block):
    up, down = [block], [block]
    for _ in range(3):
        up.append(shift(up[-1], "z", -1))
        down.append(shift(down[-1], "z", 1))
    half = T // 2
    far = jnp.concatenate([shift(up[3][:half], "z", -1), shift(down[3][half:], "z", 1)], axis=0)
    return [block, up[1], up[2], up[3], far, down[3], down[2], down[1]]


def scatter_sum_z(parts):
    half = T // 2
    up = shift(parts[4][:half], "z", 1)
    down = shift(parts[4][half:], "z", -1)
    up = jnp.concatenate([parts[3][:half] + up, parts[3][half:]], axis=0)
    down = jnp.concatenate([parts[5][:half], parts[5][half:] + down], axis=0)
    up, down = shift(up, "z", 1), shift(down, "z", -1)
    for k in (2, 1):
        up = shift(parts[k] + up, "z", 1)
        down = shift(parts[NZ - k] + down, "z", -1)
    return up, down


def across(buffers):
    a0, p1, p2, m2, m3 = buffers
    p2, m2 = shift(p2, "x", 1), shift(m2, "x", -1)
    p1, m3 = shift(p1, "x", 1), shift(m3, "x", -1)
    p2, m2 = shift(p2, "x", 1), shift(m2, "x", -1)
    return [a0, p1, p2, m2, m3]


def back(buffers):
    a0, p1, p2, m2, m3 = buffers
    p2, m2 = shift(p2, "x", -1), shift(m2, "x", 1)
    p1, m3 = shift(p1, "x", -1), shift(m3, "x", 1)
    p2, m2 = shift(p2, "x", -1), shift(m2, "x", 1)
    return [a0, p1, p2, m2, m3]


def shards(
    queries, keys, values, residual_in, attn_gain, out_proj, ffn_gain,
    w_gate, w_up, w_down, routes, gates,
):
    x, z, c = lax.axis_index("x"), lax.axis_index("z"), lax.axis_index("c")
    queries, keys, values = queries[0], keys[0], values[0]
    weight = lax.all_gather(out_proj, ("z", "c"), axis=0, tiled=True)
    states = block_states(keys, values)
    states = lax.all_to_all(states, ("x", "y"), 0, 0, tiled=True)
    prefix_low = lax.all_to_all(exclusive_prefix(states), ("x", "y"), 0, 0, tiled=True)
    local = local_parts(queries, keys, values)
    select, weights = route_tables(routes, gates, x, z, c)
    pieces = [join_pieces(w[0]) for w in (w_gate, w_up, w_down)]
    residual_sum, normed = project(
        queries, local, prefix_low, attn_gain[None], weight, residual_in[0], ffn_gain[None]
    )
    blocks = []
    for block in gather_z(normed):
        blocks += [block, shift(block, "c", 1)]
    arrived = across(pick_rows(select, blocks))
    results = experts_apply(arrived, pieces[0] + pieces[1] + pieces[2])
    own, other = mix_rows(weights, back(results))
    other = shift(other, "c", 1)
    parts = [own[k * T : (k + 1) * T].astype(F32) + other[k * T : (k + 1) * T] for k in range(NZ)]
    parts = [p.astype(BF) for p in parts]
    up, down = scatter_sum_z(parts)
    mixture = parts[0].astype(F32) + up.astype(F32) + down.astype(F32)
    return (residual_sum + mixture).astype(BF)[None]


def solution(mesh):
    shape = (NX, mesh.devices.shape[0] // NX, mesh.devices.shape[1] // 2, 2)
    grid = Mesh(mesh.devices.reshape(shape), ("x", "y", "z", "c"))
    tm, ep = ("x", "y"), ("z", "c")
    frames = P(ep, tm, None)
    pieces = P(ep + tm, None, None)
    placed = (frames, frames, frames, frames, P(), P(ep, None), P(), pieces, pieces, pieces, frames, frames)
    return jax.shard_map(
        shards, mesh=grid, in_specs=placed, out_specs=frames, check_vma=False
    )
```

```python
import jax
import jax.numpy as jnp
from jax import lax
from jax.experimental import pallas as pl
from jax.experimental.pallas import tpu as pltpu
from jax.sharding import Mesh
from jax.sharding import PartitionSpec as P

HEADS = 16
DH = 128
D = 2048
T = 128
BLK = 32
MOST = 4
NX = 4
NZ = 8
SLOTS = T // BLK * MOST
HID = 256
EPS = 1e-05
MIB = 1 << 20
BF = jnp.bfloat16
F32 = jnp.float32


def dot(a, b, ca=1, cb=0):
    return lax.dot_general(a, b, (((ca,), (cb,)), ((), ())), preferred_element_type=F32)


def shift(value, axis, step):
    count = lax.axis_size(axis)
    return lax.ppermute(value, axis, [(i, (i + step) % count) for i in range(count)])


TILE = 512
ANYWHERE = pl.BlockSpec(memory_space=pl.ANY)


def column_tile(rows):
    return pl.BlockSpec((rows, TILE), lambda j: (0, j))


def state_kernel(k_ref, v_ref, state_ref):
    for h in range(HEADS):
        at = slice(h * DH, (h + 1) * DH)
        state_ref[h] = dot(k_ref[:, at], v_ref[:, at], 0, 0).astype(BF)


def block_states(keys, values):
    return pl.pallas_call(
        state_kernel,
        out_shape=jax.ShapeDtypeStruct((HEADS, DH, DH), BF),
        name="block_states",
    )(keys, values)


def prefix_kernel(state_ref, out_ref):
    running = jnp.zeros((DH, DH), F32)
    for i in range(HEADS):
        out_ref[i] = running.astype(BF)
        running = running + state_ref[i].astype(F32)


def untouched(kernel, count):
    return lambda *refs: kernel(*refs[count:])


def block_prefixes(states, after):
    after = list(after)
    return pl.pallas_call(
        untouched(prefix_kernel, len(after)),
        in_specs=[ANYWHERE] * len(after) + [pl.BlockSpec(memory_space=pltpu.VMEM)],
        out_shape=jax.ShapeDtypeStruct(states.shape, BF),
        name="block_prefixes",
    )(*after, states)


def local_kernel(q_ref, k_ref, v_ref, out_ref):
    rows = lax.broadcasted_iota(jnp.int32, (T, T), 0)
    columns = lax.broadcasted_iota(jnp.int32, (T, T), 1)
    for h in range(4):
        at = slice(h * DH, (h + 1) * DH)
        scores = dot(q_ref[:, at], k_ref[:, at], 1, 1)
        scores = jnp.where(rows >= columns, scores, 0.0).astype(BF)
        out_ref[:, at] = dot(scores, v_ref[:, at])


def local_parts(queries, keys, values):
    heads = pl.BlockSpec((T, 4 * DH), lambda h: (0, h))
    return pl.pallas_call(
        local_kernel,
        grid=(HEADS // 4,),
        in_specs=[heads] * 3,
        out_specs=heads,
        out_shape=jax.ShapeDtypeStruct((T, D), F32),
        name="local_parts",
    )(queries, keys, values)


def project_kernel(
    q_ref, local_ref, prefix_ref, gain_ref, w_ref, res_ref, fgain_ref, sum_ref, normed_ref, att, acc
):
    step = pl.program_id(0)

    @pl.when(step == 0)
    def _():
        for h in range(HEADS):
            at = slice(h * DH, (h + 1) * DH)
            mixed = local_ref[:, at] + dot(q_ref[:, at], prefix_ref[h])
            scale = lax.rsqrt(jnp.mean(mixed * mixed, axis=-1, keepdims=True) + EPS)
            att[:, at] = (mixed * scale * gain_ref[:, at]).astype(BF)

    acc[step] = res_ref[...].astype(F32) + dot(att[...], w_ref[...])

    @pl.when(step == D // TILE - 1)
    def _():
        total = jnp.concatenate([acc[i] for i in range(D // TILE)], axis=1)
        norm = lax.rsqrt(jnp.mean(total * total, axis=-1, keepdims=True) + EPS)
        sum_ref[...] = total
        normed_ref[...] = (total * norm * fgain_ref[...]).astype(BF)


def project(queries, local, prefix_low, attn_gain, weight, residual, ffn_gain, after):
    after = list(after)
    whole = pl.BlockSpec((T, D), lambda j: (0, 0))
    row = pl.BlockSpec((1, D), lambda j: (0, 0))
    return pl.pallas_call(
        untouched(project_kernel, len(after)),
        grid=(D // TILE,),
        in_specs=[ANYWHERE] * len(after)
        + [
            whole,
            whole,
            pl.BlockSpec((HEADS, DH, DH), lambda j: (0, 0, 0)),
            row,
            column_tile(D),
            column_tile(T),
            row,
        ],
        out_specs=[whole, whole],
        out_shape=[jax.ShapeDtypeStruct((T, D), F32), jax.ShapeDtypeStruct((T, D), BF)],
        scratch_shapes=[pltpu.VMEM((T, D), BF), pltpu.VMEM((D // TILE, T, TILE), F32)],
        compiler_params=pltpu.CompilerParams(vmem_limit_bytes=40 * MIB),
        name="project",
    )(*after, queries, local, prefix_low, attn_gain, weight, residual, ffn_gain)


def route_tables(routes, gates, x, z, c):
    meta = jnp.concatenate([routes[0].T.astype(F32), gates[0].T], axis=0)
    meta = jnp.stack([meta, shift(meta, "c", 1)])[None]
    for step in (1, 2, 4):
        meta = jnp.concatenate([meta, shift(meta, "z", -step)], axis=0)
    meta = meta.reshape(2 * NZ, 8, T)
    picks, gains = meta[:, :MOST], meta[:, MOST:]
    offsets = jnp.arange(NX, dtype=jnp.int32)
    experts = ((2 * z + c) * NX + (x + offsets) % NX).astype(F32)
    hit = picks[:, None, :, :] == experts[None, :, None, None]
    named = jnp.any(hit, axis=2)
    gain = jnp.sum(jnp.where(hit, gains[:, None], 0.0), axis=2)
    frame = jnp.arange(T, dtype=jnp.int32)
    earlier = (frame[:, None] < frame[None, :]) & (frame[:, None] // BLK == frame[None, :] // BLK)
    rank = lax.dot_general(
        named.astype(BF), earlier.astype(BF), (((2,), (0,)), ((), ())), preferred_element_type=F32
    )
    slot = rank.astype(jnp.int32) + frame // BLK * MOST
    taken = named & (rank < MOST)
    match = taken[:, :, None, :] & (
        slot[:, :, None, :] == jnp.arange(SLOTS, dtype=jnp.int32)[None, None, :, None]
    )
    select = match.astype(BF).reshape(2 * NZ, NX * SLOTS, T)
    high = lax.reduce_precision(gain, 8, 7)
    low = gain - high
    split = [
        jnp.where(match, part[:, :, None, :], 0.0).astype(BF).reshape(2 * NZ, NX * SLOTS, T)
        for part in (high, low)
    ]
    return select, jnp.concatenate(split, axis=1)


def pick_kernel(count, s_ref, *refs):
    blocks, (a0, p1, p2, m2, m3) = refs[:count], refs[count:]
    half = count // 2
    for i in range(count):
        rows = dot(s_ref[i], blocks[i][...]).astype(BF)
        at = pl.ds(i * SLOTS, SLOTS)
        a0[at, :] = rows[:SLOTS]
        p1[at, :] = rows[SLOTS : 2 * SLOTS]
        mid = p2 if i < half else m2
        mid[pl.ds(i % half * SLOTS, SLOTS), :] = rows[2 * SLOTS : 3 * SLOTS]
        m3[at, :] = rows[3 * SLOTS :]


def row_counts(count):
    full, half = count * SLOTS, count // 2 * SLOTS
    return (full, full, half, half, full)


def pick_rows(select, blocks):
    count = len(blocks)
    sizes = row_counts(count)
    return pl.pallas_call(
        lambda *refs: pick_kernel(count, *refs),
        grid=(D // TILE,),
        in_specs=[pl.BlockSpec((count, NX * SLOTS, T), lambda j: (0, 0, 0))]
        + [column_tile(T)] * count,
        out_specs=[column_tile(n) for n in sizes],
        out_shape=[jax.ShapeDtypeStruct((n, D), BF) for n in sizes],
        compiler_params=pltpu.CompilerParams(vmem_limit_bytes=40 * MIB),
        name="pick_rows",
    )(select, *blocks)


def mix_kernel(count, t_ref, a0, p1, p2, m2, m3, *outs):
    half = count // 2
    for i in range(count):
        at = pl.ds(i * SLOTS, SLOTS)
        mid = p2 if i < half else m2
        rows = jnp.concatenate(
            [a0[at, :], p1[at, :], mid[pl.ds(i % half * SLOTS, SLOTS), :], m3[at, :]], axis=0
        )
        rows = jnp.concatenate([rows, rows], axis=0)
        outs[i % 2][pl.ds(i // 2 * T, T), :] = dot(t_ref[i], rows, 0, 0).astype(BF)


def mix_rows(weights, buffers):
    count = weights.shape[0]
    rows = count // 2 * T
    return pl.pallas_call(
        lambda *refs: mix_kernel(count, *refs),
        grid=(D // TILE,),
        in_specs=[pl.BlockSpec((count, 2 * NX * SLOTS, T), lambda j: (0, 0, 0))]
        + [column_tile(n) for n in row_counts(count)],
        out_specs=[column_tile(rows)] * 2,
        out_shape=[jax.ShapeDtypeStruct((rows, D), BF)] * 2,
        compiler_params=pltpu.CompilerParams(vmem_limit_bytes=40 * MIB),
        name="mix_rows",
    )(weights, *buffers)


def expert_kernel(sizes, at_y, *refs):
    n_in = len(sizes)
    inputs, weights = refs[:n_in], refs[n_in : n_in + 11]
    outs = refs[n_in + 11 : n_in + 11 + n_in]
    x_buf, g_buf, u_buf, d_buf, h_buf, o_buf, x_sem, g_sem, u_sem, d_sem, o_sem = refs[2 * n_in + 11 :]
    starts = [sum(sizes[:i]) for i in range(n_in)]
    rows = sum(sizes)
    half = D // 2
    targets = [(0, 0, D), (1, 0, D), (2, 0, D), (3, 0, half), (3, half, half)]
    x_copies = [
        pltpu.make_async_copy(inputs[i], x_buf.at[pl.ds(starts[i], sizes[i])], x_sem.at[i])
        for i in range(n_in)
    ]

    def up_copies(first_ref, buf, sem):
        return [
            pltpu.make_async_copy(weights[first_ref + i], buf.at[g, pl.ds(first, size)], sem.at[i])
            for i, (g, first, size) in enumerate(targets)
        ]

    g_copies, u_copies = up_copies(0, g_buf, g_sem), up_copies(5, u_buf, u_sem)
    d_copies = []
    for i, offset in enumerate((0, 3, 1, 2)):
        source = pl.multiple_of(lax.rem(at_y[0] + offset, 4) * HID, HID)
        d_copies.append(
            pltpu.make_async_copy(
                weights[10].at[pl.ds(source, HID)], d_buf.at[pl.ds(i * HID, HID)], d_sem.at[i]
            )
        )
    for copy in x_copies:
        copy.start()
    for i in range(5):
        g_copies[i].start()
        u_copies[i].start()
    for copy in d_copies:
        copy.start()
    for copy in x_copies:
        copy.wait()
    step = 256
    for g in range(4):
        for i in ([g], [3, 4])[g == 3]:
            g_copies[i].wait()
            u_copies[i].wait()

        def hidden_rows(r, _):
            at = pl.ds(pl.multiple_of(r * step, step), step)
            gate = dot(x_buf[at, :], g_buf[g])
            up = dot(x_buf[at, :], u_buf[g])
            h_buf[at, pl.ds(g * HID, HID)] = (gate / (1.0 + jnp.exp(-gate)) * up).astype(BF)
            return 0

        lax.fori_loop(0, rows // step, hidden_rows, 0)
    for copy in d_copies:
        copy.wait()

    def out_rows(r, _):
        at = pl.ds(pl.multiple_of(r * 128, 128), 128)
        o_buf[at, :] = dot(h_buf[at, :], d_buf[...]).astype(BF)
        return 0

    o_copies = []
    for i in range(n_in):
        lax.fori_loop(starts[i] // 128, (starts[i] + sizes[i]) // 128, out_rows, 0)
        copy = pltpu.make_async_copy(o_buf.at[pl.ds(starts[i], sizes[i])], outs[i], o_sem.at[i])
        copy.start()
        o_copies.append(copy)
    for copy in o_copies:
        copy.wait()


def experts_apply(at_y, buffers, weights):
    sizes = tuple(b.shape[0] for b in buffers)
    rows = sum(sizes)
    return pl.pallas_call(
        lambda *refs: expert_kernel(sizes, *refs),
        in_specs=[pl.BlockSpec(memory_space=pltpu.SMEM)] + [ANYWHERE] * (len(sizes) + 11),
        out_specs=[ANYWHERE] * len(sizes),
        out_shape=[jax.ShapeDtypeStruct((n, D), BF) for n in sizes],
        scratch_shapes=[
            pltpu.VMEM((rows, D), BF),
            pltpu.VMEM((4, D, HID), BF),
            pltpu.VMEM((4, D, HID), BF),
            pltpu.VMEM((4 * HID, D), BF),
            pltpu.VMEM((rows, 4 * HID), BF),
            pltpu.VMEM((rows, D), BF),
            pltpu.SemaphoreType.DMA((len(sizes),)),
            pltpu.SemaphoreType.DMA((5,)),
            pltpu.SemaphoreType.DMA((5,)),
            pltpu.SemaphoreType.DMA((4,)),
            pltpu.SemaphoreType.DMA((len(sizes),)),
        ],
        compiler_params=pltpu.CompilerParams(vmem_limit_bytes=48 * MIB),
        name="experts",
    )(at_y, *buffers, *weights)


def join_pieces(piece):
    half = piece.shape[0] // 2
    below, above = shift(piece, "y", 1), shift(piece, "y", -1)
    far_first = shift(below[:half], "y", 1)
    far_second = shift(above[half:], "y", -1)
    return [piece, below, above, far_first, far_second]


def gather_z(block):
    up, down = [block], [block]
    for _ in range(3):
        up.append(shift(up[-1], "z", -1))
        down.append(shift(down[-1], "z", 1))
    half = T // 2
    far = jnp.concatenate([shift(up[3][:half], "z", -1), shift(down[3][half:], "z", 1)], axis=0)
    return [block, up[1], up[2], up[3], far, down[3], down[2], down[1]]


def scatter_sum_z(parts):
    half = T // 2
    up = shift(parts[4][:half], "z", 1)
    down = shift(parts[4][half:], "z", -1)
    up = jnp.concatenate([parts[3][:half] + up, parts[3][half:]], axis=0)
    down = jnp.concatenate([parts[5][:half], parts[5][half:] + down], axis=0)
    up, down = shift(up, "z", 1), shift(down, "z", -1)
    for k in (2, 1):
        up = shift(parts[k] + up, "z", 1)
        down = shift(parts[NZ - k] + down, "z", -1)
    return up, down


def across(buffers):
    a0, p1, p2, m2, m3 = buffers
    p2, m2 = shift(p2, "x", 1), shift(m2, "x", -1)
    p1, m3 = shift(p1, "x", 1), shift(m3, "x", -1)
    p2, m2 = shift(p2, "x", 1), shift(m2, "x", -1)
    return [a0, p1, p2, m2, m3]


def back(buffers):
    a0, p1, p2, m2, m3 = buffers
    p2, m2 = shift(p2, "x", -1), shift(m2, "x", 1)
    p1, m3 = shift(p1, "x", -1), shift(m3, "x", 1)
    p2, m2 = shift(p2, "x", -1), shift(m2, "x", 1)
    return [a0, p1, p2, m2, m3]


def shards(
    queries, keys, values, residual_in, attn_gain, out_proj, ffn_gain,
    w_gate, w_up, w_down, routes, gates,
):
    x, y, z, c = (lax.axis_index(name) for name in ("x", "y", "z", "c"))
    queries, keys, values = queries[0], keys[0], values[0]
    weight = lax.all_gather(out_proj, ("z", "c"), axis=0, tiled=True)
    down = lax.all_gather(w_down[0], "y", axis=0, tiled=True)
    gate_pieces, up_pieces = join_pieces(w_gate[0]), join_pieces(w_up[0])
    states = block_states(keys, values)
    states = lax.all_to_all(states, ("x", "y"), 0, 0, tiled=True)
    prefix_low = block_prefixes(states, gate_pieces[1:3])
    prefix_low = lax.all_to_all(prefix_low, ("x", "y"), 0, 0, tiled=True)
    local = local_parts(queries, keys, values)
    select, weights = route_tables(routes, gates, x, z, c)
    residual_sum, normed = project(
        queries, local, prefix_low, attn_gain[None], weight, residual_in[0], ffn_gain[None],
        [select, weights] + gate_pieces[3:] + up_pieces[1:],
    )
    blocks = []
    for block in gather_z(normed):
        blocks += [block, shift(block, "c", 1)]
    arrived = across(pick_rows(select, blocks))
    results = experts_apply(y[None].astype(jnp.int32), arrived, gate_pieces + up_pieces + [down])
    own, other = mix_rows(weights, back(results))
    other = shift(other, "c", 1)
    parts = [own[k * T : (k + 1) * T].astype(F32) + other[k * T : (k + 1) * T] for k in range(NZ)]
    parts = [p.astype(BF) for p in parts]
    up, down = scatter_sum_z(parts)
    mixture = parts[0].astype(F32) + up.astype(F32) + down.astype(F32)
    return (residual_sum + mixture).astype(BF)[None]


def solution(mesh):
    shape = (NX, mesh.devices.shape[0] // NX, mesh.devices.shape[1] // 2, 2)
    grid = Mesh(mesh.devices.reshape(shape), ("x", "y", "z", "c"))
    tm, ep = ("x", "y"), ("z", "c")
    frames = P(ep, tm, None)
    pieces = P(ep + tm, None, None)
    placed = (frames, frames, frames, frames, P(), P(ep, None), P(), pieces, pieces, pieces, frames, frames)
    return jax.shard_map(
        shards, mesh=grid, in_specs=placed, out_specs=frames, check_vma=False
    )
```

```python
import jax
import jax.numpy as jnp
from jax import lax
from jax.experimental import pallas as pl
from jax.experimental.pallas import tpu as pltpu
from jax.sharding import Mesh
from jax.sharding import PartitionSpec as P

HEADS = 16
DH = 128
D = 2048
T = 128
BLK = 32
MOST = 4
NX = 4
NZ = 8
SLOTS = T // BLK * MOST
HID = 256
EPS = 1e-05
MIB = 1 << 20
BF = jnp.bfloat16
F32 = jnp.float32


def dot(a, b, ca=1, cb=0):
    return lax.dot_general(a, b, (((ca,), (cb,)), ((), ())), preferred_element_type=F32)


def shift(value, axis, step):
    count = lax.axis_size(axis)
    return lax.ppermute(value, axis, [(i, (i + step) % count) for i in range(count)])


TILE = 512
ANYWHERE = pl.BlockSpec(memory_space=pl.ANY)
TOKEN = jax.ShapeDtypeStruct((8, 128), F32)
TOKEN_SPEC = pl.BlockSpec((8, 128), lambda j: (0, 0))


def column_tile(rows):
    return pl.BlockSpec((rows, TILE), lambda j: (0, j))


def state_kernel(k_ref, v_ref, state_ref):
    for h in range(HEADS):
        at = slice(h * DH, (h + 1) * DH)
        state_ref[h] = dot(k_ref[:, at], v_ref[:, at], 0, 0)


def block_states(keys, values):
    return pl.pallas_call(
        state_kernel,
        out_shape=jax.ShapeDtypeStruct((HEADS, DH, DH), F32),
        name="block_states",
    )(keys, values)


def prefix_kernel(state_ref, out_ref):
    running = jnp.zeros((DH, DH), F32)
    for i in range(HEADS):
        out_ref[i] = running.astype(BF)
        running = running + state_ref[i]


def untouched(kernel, count):
    return lambda *refs: kernel(*refs[count:])


def block_prefixes(states, after):
    after = list(after)
    return pl.pallas_call(
        untouched(prefix_kernel, len(after)),
        in_specs=[ANYWHERE] * len(after) + [pl.BlockSpec(memory_space=pltpu.VMEM)],
        out_shape=jax.ShapeDtypeStruct(states.shape, BF),
        name="block_prefixes",
    )(*after, states)


def held_kernel(value_ref, after_ref, out_ref, sem):
    copy = pltpu.make_async_copy(value_ref, out_ref, sem)
    copy.start()
    copy.wait()


def held(value, after):
    return pl.pallas_call(
        held_kernel,
        in_specs=[ANYWHERE] * 2,
        out_specs=ANYWHERE,
        out_shape=jax.ShapeDtypeStruct(value.shape, value.dtype),
        scratch_shapes=[pltpu.SemaphoreType.DMA],
        name="held",
    )(value, after)


def tied(value, after):
    after = list(after)
    return pl.pallas_call(
        lambda *refs: None,
        in_specs=[ANYWHERE] * (1 + len(after)),
        out_specs=ANYWHERE,
        out_shape=jax.ShapeDtypeStruct(value.shape, value.dtype),
        input_output_aliases={0: 0},
        name="tied",
    )(value, *after)


def local_kernel(q_ref, k_ref, v_ref, out_ref):
    rows = lax.broadcasted_iota(jnp.int32, (T, T), 0)
    columns = lax.broadcasted_iota(jnp.int32, (T, T), 1)
    for h in range(4):
        at = slice(h * DH, (h + 1) * DH)
        scores = dot(q_ref[:, at], k_ref[:, at], 1, 1)
        scores = jnp.where(rows >= columns, scores, 0.0).astype(BF)
        out_ref[:, at] = dot(scores, v_ref[:, at])


def local_parts(queries, keys, values):
    heads = pl.BlockSpec((T, 4 * DH), lambda h: (0, h))
    return pl.pallas_call(
        local_kernel,
        grid=(HEADS // 4,),
        in_specs=[heads] * 3,
        out_specs=heads,
        out_shape=jax.ShapeDtypeStruct((T, D), F32),
        name="local_parts",
    )(queries, keys, values)


def project_kernel(
    q_ref, local_ref, prefix_ref, gain_ref, w_ref, res_ref, fgain_ref, sum_ref, normed_ref, att, acc
):
    step = pl.program_id(0)

    @pl.when(step == 0)
    def _():
        for h in range(HEADS):
            at = slice(h * DH, (h + 1) * DH)
            mixed = local_ref[:, at] + dot(q_ref[:, at], prefix_ref[h])
            scale = lax.rsqrt(jnp.mean(mixed * mixed, axis=-1, keepdims=True) + EPS)
            att[:, at] = (mixed * scale * gain_ref[:, at]).astype(BF)

    acc[step] = res_ref[...].astype(F32) + dot(att[...], w_ref[...])

    @pl.when(step == D // TILE - 1)
    def _():
        total = jnp.concatenate([acc[i] for i in range(D // TILE)], axis=1)
        norm = lax.rsqrt(jnp.mean(total * total, axis=-1, keepdims=True) + EPS)
        sum_ref[...] = total
        normed_ref[...] = (total * norm * fgain_ref[...]).astype(BF)


def project(queries, local, prefix_low, attn_gain, weight, residual, ffn_gain, after):
    after = list(after)
    whole = pl.BlockSpec((T, D), lambda j: (0, 0))
    row = pl.BlockSpec((1, D), lambda j: (0, 0))
    return pl.pallas_call(
        untouched(project_kernel, len(after)),
        grid=(D // TILE,),
        in_specs=[ANYWHERE] * len(after)
        + [
            whole,
            whole,
            pl.BlockSpec((HEADS, DH, DH), lambda j: (0, 0, 0)),
            row,
            column_tile(D),
            column_tile(T),
            row,
        ],
        out_specs=[whole, whole],
        out_shape=[jax.ShapeDtypeStruct((T, D), F32), jax.ShapeDtypeStruct((T, D), BF)],
        scratch_shapes=[pltpu.VMEM((T, D), BF), pltpu.VMEM((D // TILE, T, TILE), F32)],
        compiler_params=pltpu.CompilerParams(vmem_limit_bytes=20 * MIB),
        name="project",
    )(*after, queries, local, prefix_low, attn_gain, weight, residual, ffn_gain)


def route_tables(meta, z, c):
    meta = jnp.stack([meta, shift(meta, "c", 1)])[None]
    for step in (1, 2, 4):
        meta = jnp.concatenate([meta, shift(meta, "z", -step)], axis=0)
    meta = meta.reshape(2 * NZ, 8, T)
    picks, gains = meta[:, :MOST], meta[:, MOST:]
    offsets = jnp.arange(NX, dtype=jnp.int32)
    experts = ((2 * z + c) * NX + offsets).astype(F32)
    hit = picks[:, None, :, :] == experts[None, :, None, None]
    named = jnp.any(hit, axis=2)
    gain = jnp.sum(jnp.where(hit, gains[:, None], 0.0), axis=2)
    frame = jnp.arange(T, dtype=jnp.int32)
    earlier = (frame[:, None] < frame[None, :]) & (frame[:, None] // BLK == frame[None, :] // BLK)
    rank = lax.dot_general(
        named.astype(BF), earlier.astype(BF), (((2,), (0,)), ((), ())), preferred_element_type=F32
    )
    slot = rank.astype(jnp.int32) + frame // BLK * MOST
    taken = named & (rank < MOST)
    match = taken[:, :, None, :] & (
        slot[:, :, None, :] == jnp.arange(SLOTS, dtype=jnp.int32)[None, None, :, None]
    )
    select = match.astype(BF).reshape(2 * NZ, NX * SLOTS, T)
    high = lax.reduce_precision(gain, 8, 7)
    low = gain - high
    split = [
        jnp.where(match, part[:, :, None, :], 0.0).astype(BF).reshape(2 * NZ, NX * SLOTS, T)
        for part in (high, low)
    ]
    return select, jnp.concatenate(split, axis=1)


def pick_kernel(count, s_ref, *refs):
    out, token = refs[count:]
    token[...] = jnp.zeros_like(token)
    for i in range(count):
        rows = dot(s_ref[i], refs[i][...]).astype(BF)
        for j in range(NX):
            out[j, pl.ds(i * SLOTS, SLOTS), :] = rows[j * SLOTS : (j + 1) * SLOTS]


def slot_tile(count):
    return pl.BlockSpec((NX, count * SLOTS, TILE), lambda j: (0, 0, j))


def pick_rows(select, blocks, after):
    count = len(blocks)
    after = list(after)
    return pl.pallas_call(
        untouched(lambda *refs: pick_kernel(count, *refs), len(after)),
        grid=(D // TILE,),
        in_specs=[ANYWHERE] * len(after) + [pl.BlockSpec((count, NX * SLOTS, T), lambda j: (0, 0, 0))]
        + [column_tile(T)] * count,
        out_specs=[slot_tile(count), TOKEN_SPEC],
        out_shape=[jax.ShapeDtypeStruct((NX, count * SLOTS, D), BF), TOKEN],
        name="pick_rows",
    )(*after, select, *blocks)


def mix_kernel(count, first, t_ref, rows_ref, own_ref, other_ref):
    for i in range(count):
        at = pl.ds((first + i) * SLOTS, SLOTS)
        rows = jnp.concatenate([rows_ref[j, at, :] for j in range(NX)] * 2, axis=0)
        out = other_ref if i % 2 else own_ref
        out[pl.ds(i // 2 * T, T), :] = dot(t_ref[i], rows, 0, 0).astype(BF)


def mix_rows(weights, rows, first, after):
    count = weights.shape[0]
    after = list(after)
    frames = count // 2 * T
    return pl.pallas_call(
        untouched(lambda *refs: mix_kernel(count, first, *refs), len(after)),
        grid=(D // TILE,),
        in_specs=[ANYWHERE] * len(after) + [pl.BlockSpec((count, 2 * NX * SLOTS, T), lambda j: (0, 0, 0)), slot_tile(rows.shape[1] // SLOTS)],
        out_specs=[column_tile(frames)] * 2,
        out_shape=[jax.ShapeDtypeStruct((frames, D), BF)] * 2,
        name="mix_rows",
    )(*after, weights, rows)


def expert_kernel(sizes, at_y, *refs):
    n_in = len(sizes)
    inputs, weights = refs[:n_in], refs[n_in : n_in + 11]
    out, token = refs[n_in + 11 : n_in + 13]
    x_buf, g_buf, u_buf, d_buf, h_buf, o_buf, x_sem, g_sem, u_sem, d_sem, o_sem = refs[n_in + 13 :]
    token[...] = jnp.zeros_like(token)
    starts = [sum(sizes[:i]) for i in range(n_in)]
    rows = sum(sizes)
    half = D // 2
    targets = [(0, 0, D), (1, 0, D), (2, 0, D), (3, 0, half), (3, half, half)]
    x_copies = [
        pltpu.make_async_copy(inputs[i], x_buf.at[pl.ds(starts[i], sizes[i])], x_sem.at[i])
        for i in range(n_in)
    ]

    def up_copies(first_ref, buf, sem):
        return [
            pltpu.make_async_copy(weights[first_ref + i], buf.at[g, pl.ds(first, size)], sem.at[i])
            for i, (g, first, size) in enumerate(targets)
        ]

    g_copies, u_copies = up_copies(0, g_buf, g_sem), up_copies(5, u_buf, u_sem)
    d_copies = []
    for i, offset in enumerate((0, 3, 1, 2)):
        source = pl.multiple_of(lax.rem(at_y[0] + offset, 4) * HID, HID)
        d_copies.append(
            pltpu.make_async_copy(
                weights[10].at[pl.ds(source, HID)], d_buf.at[pl.ds(i * HID, HID)], d_sem.at[i]
            )
        )
    for copy in x_copies:
        copy.start()
    for i in range(5):
        g_copies[i].start()
        u_copies[i].start()
    for copy in d_copies:
        copy.start()
    for copy in x_copies:
        copy.wait()
    for g in range(4):
        for i in ([g], [3, 4])[g == 3]:
            g_copies[i].wait()
            u_copies[i].wait()
        gate = dot(x_buf[...], g_buf[g])
        up = dot(x_buf[...], u_buf[g])
        h_buf[:, g * HID : (g + 1) * HID] = (gate / (1.0 + jnp.exp(-gate)) * up).astype(BF)
    for copy in d_copies:
        copy.wait()

    def out_columns(j, _):
        at = pl.ds(pl.multiple_of(j * TILE, TILE), TILE)
        o_buf[:, at] = dot(h_buf[...], d_buf[:, at]).astype(BF)
        return 0

    lax.fori_loop(0, D // TILE, out_columns, 0)
    o_copies = []
    place = 0
    for i in range(n_in):
        part = sizes[i] // NX
        for j in range(NX):
            copy = pltpu.make_async_copy(
                o_buf.at[pl.ds(starts[i] + j * part, part)],
                out.at[j, pl.ds(place, part)],
                o_sem.at[i * NX + j],
            )
            copy.start()
            o_copies.append(copy)
        place += part
    for copy in o_copies:
        copy.wait()


def experts_apply(at_y, chunks, weights, after):
    after = list(after)
    buffers = [chunk.reshape(-1, D) for chunk in chunks]
    sizes = tuple(b.shape[0] for b in buffers)
    rows = sum(sizes)
    return pl.pallas_call(
        untouched(lambda *refs: expert_kernel(sizes, *refs), len(after)),
        in_specs=[ANYWHERE] * len(after)
        + [pl.BlockSpec(memory_space=pltpu.SMEM)]
        + [ANYWHERE] * (len(sizes) + 11),
        out_specs=[ANYWHERE, pl.BlockSpec(memory_space=pltpu.VMEM)],
        out_shape=[jax.ShapeDtypeStruct((NX, rows // NX, D), BF), TOKEN],
        scratch_shapes=[
            pltpu.VMEM((rows, D), BF),
            pltpu.VMEM((4, D, HID), BF),
            pltpu.VMEM((4, D, HID), BF),
            pltpu.VMEM((4 * HID, D), BF),
            pltpu.VMEM((rows, 4 * HID), BF),
            pltpu.VMEM((rows, D), BF),
            pltpu.SemaphoreType.DMA((len(sizes),)),
            pltpu.SemaphoreType.DMA((5,)),
            pltpu.SemaphoreType.DMA((5,)),
            pltpu.SemaphoreType.DMA((4,)),
            pltpu.SemaphoreType.DMA((len(sizes) * NX,)),
        ],
        compiler_params=pltpu.CompilerParams(vmem_limit_bytes=26 * MIB),
        name="experts",
    )(*after, at_y, *buffers, *weights)


def join_pieces(piece):
    half = piece.shape[0] // 2
    below, above = shift(piece, "y", 1), shift(piece, "y", -1)
    far_first = shift(below[:half], "y", 1)
    far_second = shift(above[half:], "y", -1)
    return [piece, below, above, far_first, far_second]


def add_kernel(has_ring, *refs):
    first, second, token = refs[-3:]
    token[...] = jnp.zeros_like(token)
    half = T // 2
    if has_ring:
        own_up, own_down, other_up, other_down, ring_up, ring_down = (r[...].astype(F32) for r in refs[:6])
        up, down = own_up + other_up, own_down + other_down
        if ring_up.shape[0] == half:
            first[pl.ds(0, half), :] = (up[:half] + ring_up).astype(BF)
            first[pl.ds(half, half), :] = up[half:].astype(BF)
            second[pl.ds(0, half), :] = down[:half].astype(BF)
            second[pl.ds(half, half), :] = (down[half:] + ring_down).astype(BF)
        else:
            first[...] = (up + ring_up).astype(BF)
            second[...] = (down + ring_down).astype(BF)
    else:
        total = (refs[0][...].astype(F32) + refs[1][...].astype(F32)).astype(BF)
        first[...] = total[:half]
        second[...] = total[half:]


def rows_at(index, rows):
    return pl.BlockSpec((rows, D), lambda i: (index, 0))


def ring_add(own, other, places, ring):
    specs = [rows_at(place, T) for place in places] * 2
    rows = T if ring else T // 2
    args = [own] * len(places) + [other] * len(places)
    if ring:
        specs += [rows_at(0, ring[0].shape[0])] * 2
        args += ring
    return pl.pallas_call(
        lambda *refs: add_kernel(bool(ring), *refs),
        grid=(1,),
        in_specs=specs,
        out_specs=[rows_at(0, rows)] * 2 + [TOKEN_SPEC],
        out_shape=[jax.ShapeDtypeStruct((rows, D), BF)] * 2 + [TOKEN],
        name="ring_add",
    )(*args)


def final_kernel(sum_ref, own_ref, other_ref, up_ref, down_ref, out_ref):
    mixture = own_ref[...].astype(F32) + other_ref[...].astype(F32)
    mixture = mixture + up_ref[...].astype(F32) + down_ref[...].astype(F32)
    out_ref[...] = (sum_ref[...] + mixture).astype(BF)


def final_sum(residual_sum, own, other, up, down):
    return pl.pallas_call(
        final_kernel,
        grid=(1,),
        in_specs=[rows_at(0, T)] + [rows_at(1, T)] * 2 + [rows_at(0, T)] * 2,
        out_specs=rows_at(0, T),
        out_shape=jax.ShapeDtypeStruct((T, D), BF),
        name="final_sum",
    )(residual_sum, own, other, up, down)


CHUNKS = ((1, 0, 7), (2, 6), (3, 4, 5))


def shards(
    queries, keys, values, residual_in, attn_gain, out_proj, ffn_gain,
    w_gate, w_up, w_down, routes, gates,
):
    y, z, c = (lax.axis_index(name) for name in ("y", "z", "c"))
    queries, keys, values = queries[0], keys[0], values[0]
    weight = lax.all_gather(out_proj, ("z", "c"), axis=0, tiled=True)
    down = lax.all_gather(w_down[0], "y", axis=0, tiled=True)
    gate_pieces = join_pieces(w_gate[0])
    states = block_states(keys, values)
    meta = held(jnp.concatenate([routes[0].T.astype(F32), gates[0].T], axis=0), states)
    states = lax.all_to_all(states, ("x", "y"), 0, 0, tiled=True)
    prefix_low = block_prefixes(states, gate_pieces[1:3])
    up_pieces = join_pieces(held(w_up[0], prefix_low))
    prefix_low = lax.all_to_all(prefix_low, ("x", "y"), 0, 0, tiled=True)
    local = local_parts(queries, keys, values)
    select, weights = route_tables(meta, z, c)
    select = [select[i] for i in range(2 * NZ)]
    weights = [weights[i] for i in range(2 * NZ)]
    tables = [
        [jnp.stack([table[2 * k + p] for k in chunk for p in range(2)]) for table in (select, weights)]
        for chunk in CHUNKS
    ]
    residual_sum, normed = project(
        queries, local, prefix_low, attn_gain[None], weight, residual_in[0], ffn_gain[None],
        [t for pair in tables for t in pair] + gate_pieces[3:] + up_pieces[1:3],
    )
    half = T // 2
    blocks = [normed] + [None] * (NZ - 1)
    arrived, token = [], None
    for chunk, (chosen, _) in zip(CHUNKS, tables):
        near = chunk[0]
        up, down_block = blocks[near - 1], blocks[1 - near]
        if token is not None:
            up = blocks[near - 1] = tied(up, [token])
        blocks[near], blocks[NZ - near] = shift(up, "z", -1), shift(down_block, "z", 1)
        if near == 3:
            far = [shift(blocks[3][:half], "z", -1), shift(blocks[5][half:], "z", 1)]
            blocks[4] = jnp.concatenate(far, axis=0)
        pairs = [b for k in chunk for b in (blocks[k], shift(blocks[k], "c", 1))]
        after = [[], up_pieces[3:], [token]][len(arrived)]
        picked, token = pick_rows(chosen, pairs, after)
        arrived.append(lax.all_to_all(picked, "x", 0, 0, tiled=True))
    pieces = gate_pieces + up_pieces + [down]
    at_y = y[None].astype(jnp.int32)
    near, token = experts_apply(at_y, arrived[:2], pieces, [token])
    far, _ = experts_apply(at_y, arrived[2:], pieces, [token])
    far = lax.all_to_all(far, "x", 0, 0, tiled=True)
    near = lax.all_to_all(tied(near, [far]), "x", 0, 0, tiled=True)
    own, other = {}, {}

    def mix(chunk, rows, first, after):
        own[chunk], theirs = mix_rows(tables[chunk][1], rows, first, after)
        other[chunk] = shift(theirs, "c", 1)

    def pass_on(chunk, places, ring):
        up, down, token = ring_add(own[chunk], other[chunk], places, ring)
        return [shift(up, "z", 1), shift(down, "z", -1)], [token]

    mix(2, far, 0, [])
    ring, done = pass_on(2, (1,), [])
    ring, done = pass_on(2, (0, 2), ring)
    mix(1, near, 2 * len(CHUNKS[0]), done)
    mix(0, near, 0, done)
    ring, done = pass_on(1, (0, 1), ring)
    ring, done = pass_on(0, (0, 2), ring)
    return final_sum(residual_sum, own[0], other[0], *ring)[None]


def solution(mesh):
    shape = (NX, mesh.devices.shape[0] // NX, mesh.devices.shape[1] // 2, 2)
    grid = Mesh(mesh.devices.reshape(shape), ("x", "y", "z", "c"))
    tm, ep = ("x", "y"), ("z", "c")
    frames = P(ep, tm, None)
    pieces = P(ep + tm, None, None)
    placed = (frames, frames, frames, frames, P(), P(ep, None), P(), pieces, pieces, pieces, frames, frames)
    return jax.shard_map(
        shards, mesh=grid, in_specs=placed, out_specs=frames, check_vma=False
    )
```

```python
import jax
import jax.numpy as jnp
from jax import lax
from jax.experimental import pallas as pl
from jax.experimental.pallas import tpu as pltpu
from jax.sharding import Mesh
from jax.sharding import PartitionSpec as P

HEADS = 16
DH = 128
D = 2048
T = 128
BLK = 32
MOST = 4
NX = 4
NZ = 8
SLOTS = T // BLK * MOST
HID = 256
EPS = 1e-05
MIB = 1 << 20
BF = jnp.bfloat16
F32 = jnp.float32


def dot(a, b, ca=1, cb=0):
    return lax.dot_general(a, b, (((ca,), (cb,)), ((), ())), preferred_element_type=F32)


def shift(value, axis, step):
    count = lax.axis_size(axis)
    return lax.ppermute(value, axis, [(i, (i + step) % count) for i in range(count)])


TILE = 512
ANYWHERE = pl.BlockSpec(memory_space=pl.ANY)
UNREAD = pl.BlockSpec(memory_space=pltpu.HBM)
ON_CHIP = pl.BlockSpec(memory_space=pltpu.VMEM)
TOKEN = jax.ShapeDtypeStruct((8, 128), F32)
TOKEN_SPEC = pl.BlockSpec((8, 128), lambda j: (0, 0))


def column_tile(rows):
    return pl.BlockSpec((rows, TILE), lambda j: (0, j))


def state_kernel(k_ref, v_ref, state_ref):
    for h in range(HEADS):
        at = slice(h * DH, (h + 1) * DH)
        state_ref[h] = dot(k_ref[:, at], v_ref[:, at], 0, 0)


def block_states(keys, values):
    return pl.pallas_call(
        state_kernel,
        out_shape=jax.ShapeDtypeStruct((HEADS, DH, DH), F32),
        name="block_states",
    )(keys, values)


def prefix_kernel(state_ref, out_ref):
    running = jnp.zeros((DH, DH), F32)
    for i in range(HEADS):
        out_ref[i] = running.astype(BF)
        running = running + state_ref[i]


def corner(value):
    return lax.slice(value, (0,) * value.ndim, (1,) * (value.ndim - 2) + (16, 128))


def untouched(kernel, count):
    return lambda *refs: kernel(*refs[count:])


def block_prefixes(states, after):
    after = [corner(v) if v.size > 1024 else v for v in after]
    return pl.pallas_call(
        untouched(prefix_kernel, len(after)),
        in_specs=[UNREAD] * len(after) + [pl.BlockSpec(memory_space=pltpu.VMEM)],
        out_shape=jax.ShapeDtypeStruct(states.shape, BF),
        name="block_prefixes",
    )(*after, states)


def token_kernel(*refs):
    refs[-1][...] = jnp.zeros_like(refs[-1])


def token_after(after):
    after = [corner(v) for v in after]
    return pl.pallas_call(
        token_kernel,
        in_specs=[UNREAD] * len(after),
        out_shape=TOKEN,
        name="token_after",
    )(*after)


def held(value, token):
    return jnp.where(token[0, 0] == 0.0, value, jnp.zeros_like(value))


def tied(value, after):
    after = [corner(v) if v.size > 1024 else v for v in after]
    return pl.pallas_call(
        lambda *refs: None,
        in_specs=[ANYWHERE] + [UNREAD] * len(after),
        out_specs=ANYWHERE,
        out_shape=jax.ShapeDtypeStruct(value.shape, value.dtype),
        input_output_aliases={0: 0},
        name="tied",
    )(value, *after)


def local_kernel(q_ref, k_ref, v_ref, out_ref):
    rows = lax.broadcasted_iota(jnp.int32, (T, T), 0)
    columns = lax.broadcasted_iota(jnp.int32, (T, T), 1)
    for h in range(4):
        at = slice(h * DH, (h + 1) * DH)
        scores = dot(q_ref[:, at], k_ref[:, at], 1, 1)
        scores = jnp.where(rows >= columns, scores, 0.0).astype(BF)
        out_ref[:, at] = dot(scores, v_ref[:, at])


def local_parts(queries, keys, values):
    heads = pl.BlockSpec((T, 4 * DH), lambda h: (0, h))
    return pl.pallas_call(
        local_kernel,
        grid=(HEADS // 4,),
        in_specs=[heads] * 3,
        out_specs=heads,
        out_shape=jax.ShapeDtypeStruct((T, D), F32),
        name="local_parts",
    )(queries, keys, values)


def project_kernel(
    q_ref, local_ref, prefix_ref, gain_ref, w_ref, res_ref, fgain_ref, sum_ref, normed_ref, att, acc
):
    step = pl.program_id(0)

    @pl.when(step == 0)
    def _():
        for h in range(HEADS):
            at = slice(h * DH, (h + 1) * DH)
            mixed = local_ref[:, at] + dot(q_ref[:, at], prefix_ref[h])
            scale = lax.rsqrt(jnp.mean(mixed * mixed, axis=-1, keepdims=True) + EPS)
            att[:, at] = (mixed * scale * gain_ref[:, at]).astype(BF)

    acc[step] = res_ref[...].astype(F32) + dot(att[...], w_ref[...])

    @pl.when(step == D // TILE - 1)
    def _():
        total = jnp.concatenate([acc[i] for i in range(D // TILE)], axis=1)
        norm = lax.rsqrt(jnp.mean(total * total, axis=-1, keepdims=True) + EPS)
        sum_ref[...] = total
        normed_ref[...] = (total * norm * fgain_ref[...]).astype(BF)


def project(queries, local, prefix_low, attn_gain, weight, residual, ffn_gain, after):
    after = [corner(v) if v.size > 1024 else v for v in after]
    whole = pl.BlockSpec((T, D), lambda j: (0, 0))
    row = pl.BlockSpec((1, D), lambda j: (0, 0))
    weight = pltpu.with_memory_space_constraint(weight, pltpu.HBM)
    return pl.pallas_call(
        untouched(project_kernel, len(after)),
        grid=(D // TILE,),
        in_specs=[UNREAD] * len(after)
        + [
            whole,
            whole,
            pl.BlockSpec((HEADS, DH, DH), lambda j: (0, 0, 0)),
            row,
            column_tile(D),
            column_tile(T),
            row,
        ],
        out_specs=[whole, whole],
        out_shape=[jax.ShapeDtypeStruct((T, D), F32), jax.ShapeDtypeStruct((T, D), BF)],
        scratch_shapes=[pltpu.VMEM((T, D), BF), pltpu.VMEM((D // TILE, T, TILE), F32)],
        compiler_params=pltpu.CompilerParams(vmem_limit_bytes=20 * MIB),
        name="project",
    )(*after, queries, local, prefix_low, attn_gain, weight, residual, ffn_gain)


def route_tables(meta, z, c):
    meta = jnp.stack([meta, shift(meta, "c", 1)])[None]
    for step in (1, 2, 4):
        meta = jnp.concatenate([meta, shift(meta, "z", -step)], axis=0)
    meta = meta.reshape(2 * NZ, 8, T)
    picks, gains = meta[:, :MOST], meta[:, MOST:]
    offsets = jnp.arange(NX, dtype=jnp.int32)
    experts = ((2 * z + c) * NX + offsets).astype(F32)
    hit = picks[:, None, :, :] == experts[None, :, None, None]
    named = jnp.any(hit, axis=2)
    gain = jnp.sum(jnp.where(hit, gains[:, None], 0.0), axis=2)
    frame = jnp.arange(T, dtype=jnp.int32)
    earlier = (frame[:, None] < frame[None, :]) & (frame[:, None] // BLK == frame[None, :] // BLK)
    rank = lax.dot_general(
        named.astype(BF), earlier.astype(BF), (((2,), (0,)), ((), ())), preferred_element_type=F32
    )
    slot = rank.astype(jnp.int32) + frame // BLK * MOST
    taken = named & (rank < MOST)
    match = taken[:, :, None, :] & (
        slot[:, :, None, :] == jnp.arange(SLOTS, dtype=jnp.int32)[None, None, :, None]
    )
    select = match.astype(BF).reshape(2 * NZ, NX * SLOTS, T)
    high = lax.reduce_precision(gain, 8, 7)
    low = gain - high
    split = [
        jnp.where(match, part[:, :, None, :], 0.0).astype(BF).reshape(2 * NZ, NX * SLOTS, T)
        for part in (high, low)
    ]
    return select, jnp.concatenate(split, axis=1)


def pick_kernel(count, s_ref, *refs):
    out, token = refs[count:]
    token[...] = jnp.zeros_like(token)
    for i in range(count):
        rows = dot(s_ref[i], refs[i][...]).astype(BF)
        for j in range(NX):
            out[j, pl.ds(i * SLOTS, SLOTS), :] = rows[j * SLOTS : (j + 1) * SLOTS]


def pick_rows(select, blocks, after):
    count = len(blocks)
    after = [corner(v) if v.size > 1024 else v for v in after]
    return pl.pallas_call(
        untouched(lambda *refs: pick_kernel(count, *refs), len(after)),
        in_specs=[UNREAD] * len(after) + [ON_CHIP] * (1 + count),
        out_specs=[ON_CHIP] * 2,
        out_shape=[jax.ShapeDtypeStruct((NX, count * SLOTS, D), BF), TOKEN],
        name="pick_rows",
    )(*after, select, *blocks)


def mix_kernel(count, first, t_ref, rows_ref, own_ref, other_ref):
    for i in range(count):
        at = pl.ds((first + i) * SLOTS, SLOTS)
        out = other_ref if i % 2 else own_ref
        for j in range(0, D, TILE):
            rows = jnp.concatenate([rows_ref[e, at, j : j + TILE] for e in range(NX)] * 2, axis=0)
            out[pl.ds(i // 2 * T, T), j : j + TILE] = dot(t_ref[i], rows, 0, 0).astype(BF)


def mix_rows(weights, rows, first, after):
    count = weights.shape[0]
    after = [corner(v) if v.size > 1024 else v for v in after]
    return pl.pallas_call(
        untouched(lambda *refs: mix_kernel(count, first, *refs), len(after)),
        in_specs=[UNREAD] * len(after) + [ON_CHIP] * 2,
        out_specs=[ON_CHIP] * 2,
        out_shape=[jax.ShapeDtypeStruct((count // 2 * T, D), BF)] * 2,
        name="mix_rows",
    )(*after, weights, rows)


def expert_kernel(sizes, at_y, *refs):
    n_in = len(sizes)
    inputs, weights = refs[:n_in], refs[n_in : n_in + 11]
    out, token = refs[n_in + 11 : n_in + 13]
    x_buf, g_buf, u_buf, d_buf, h_buf, o_buf, x_sem, g_sem, u_sem, d_sem, o_sem = refs[n_in + 13 :]
    token[...] = jnp.zeros_like(token)
    starts = [sum(sizes[:i]) for i in range(n_in)]
    rows = sum(sizes)
    half = D // 2
    targets = [(0, 0, D), (1, 0, D), (2, 0, D), (3, 0, half), (3, half, half)]
    x_copies = [
        pltpu.make_async_copy(inputs[i], x_buf.at[pl.ds(starts[i], sizes[i])], x_sem.at[i])
        for i in range(n_in)
    ]

    def up_copies(first_ref, buf, sem):
        return [
            pltpu.make_async_copy(weights[first_ref + i], buf.at[g, pl.ds(first, size)], sem.at[i])
            for i, (g, first, size) in enumerate(targets)
        ]

    g_copies, u_copies = up_copies(0, g_buf, g_sem), up_copies(5, u_buf, u_sem)
    d_copies = []
    for i, offset in enumerate((0, 3, 1, 2)):
        source = pl.multiple_of(lax.rem(at_y[0] + offset, 4) * HID, HID)
        d_copies.append(
            pltpu.make_async_copy(
                weights[10].at[pl.ds(source, HID)], d_buf.at[pl.ds(i * HID, HID)], d_sem.at[i]
            )
        )
    for copy in x_copies:
        copy.start()
    for i in range(5):
        g_copies[i].start()
        u_copies[i].start()
    for copy in d_copies:
        copy.start()
    for copy in x_copies:
        copy.wait()
    for g in range(4):
        for i in ([g], [3, 4])[g == 3]:
            g_copies[i].wait()
            u_copies[i].wait()
        gate = dot(x_buf[...], g_buf[g])
        up = dot(x_buf[...], u_buf[g])
        h_buf[:, g * HID : (g + 1) * HID] = (gate / (1.0 + jnp.exp(-gate)) * up).astype(BF)
    for copy in d_copies:
        copy.wait()

    def out_columns(j, _):
        at = pl.ds(pl.multiple_of(j * TILE, TILE), TILE)
        o_buf[:, at] = dot(h_buf[...], d_buf[:, at]).astype(BF)
        return 0

    lax.fori_loop(0, D // TILE, out_columns, 0)
    o_copies = []
    place = 0
    for i in range(n_in):
        part = sizes[i] // NX
        for j in range(NX):
            copy = pltpu.make_async_copy(
                o_buf.at[pl.ds(starts[i] + j * part, part)],
                out.at[j, pl.ds(place, part)],
                o_sem.at[i * NX + j],
            )
            copy.start()
            o_copies.append(copy)
        place += part
    for copy in o_copies:
        copy.wait()


def experts_apply(at_y, chunks, weights, after):
    after = [corner(v) if v.size > 1024 else v for v in after]
    buffers = [chunk.reshape(-1, D) for chunk in chunks]
    sizes = tuple(b.shape[0] for b in buffers)
    rows = sum(sizes)
    return pl.pallas_call(
        untouched(lambda *refs: expert_kernel(sizes, *refs), len(after)),
        in_specs=[UNREAD] * len(after)
        + [pl.BlockSpec(memory_space=pltpu.SMEM)]
        + [ANYWHERE] * len(sizes)
        + [UNREAD] * 11,
        out_specs=[ANYWHERE, pl.BlockSpec(memory_space=pltpu.VMEM)],
        out_shape=[jax.ShapeDtypeStruct((NX, rows // NX, D), BF), TOKEN],
        scratch_shapes=[
            pltpu.VMEM((rows, D), BF),
            pltpu.VMEM((4, D, HID), BF),
            pltpu.VMEM((4, D, HID), BF),
            pltpu.VMEM((4 * HID, D), BF),
            pltpu.VMEM((rows, 4 * HID), BF),
            pltpu.VMEM((rows, D), BF),
            pltpu.SemaphoreType.DMA((len(sizes),)),
            pltpu.SemaphoreType.DMA((5,)),
            pltpu.SemaphoreType.DMA((5,)),
            pltpu.SemaphoreType.DMA((4,)),
            pltpu.SemaphoreType.DMA((len(sizes) * NX,)),
        ],
        compiler_params=pltpu.CompilerParams(vmem_limit_bytes=26 * MIB),
        name="experts",
    )(*after, at_y, *buffers, *weights)


def join_pieces(piece):
    half = piece.shape[0] // 2
    below, above = shift(piece, "y", 1), shift(piece, "y", -1)
    far_first = shift(below[:half], "y", 1)
    far_second = shift(above[half:], "y", -1)
    return [piece, below, above, far_first, far_second]


def ring_add(own, other, places, ring):
    half = T // 2
    up, down = (
        own[p * T : (p + 1) * T].astype(F32) + other[p * T : (p + 1) * T].astype(F32)
        for p in (places[0], places[-1])
    )
    if not ring:
        return up[:half].astype(BF), down[half:].astype(BF)
    first, second = (r.astype(F32) for r in lax.optimization_barrier(tuple(ring)))
    if first.shape[0] == half:
        first = jnp.concatenate([first, jnp.zeros_like(first)], axis=0)
        second = jnp.concatenate([jnp.zeros_like(second), second], axis=0)
    return (up + first).astype(BF), (down + second).astype(BF)


def final_sum(residual_sum, own, other, up, down, place):
    at = slice(place * T, (place + 1) * T)
    mixture = own[at].astype(F32) + other[at].astype(F32) + up.astype(F32) + down.astype(F32)
    return (residual_sum + mixture).astype(BF)


CHUNKS = ((1, 0, 7), (2, 6), (3, 4, 5))


def shards(
    queries, keys, values, residual_in, attn_gain, out_proj, ffn_gain,
    w_gate, w_up, w_down, routes, gates,
):
    y, z, c = (lax.axis_index(name) for name in ("y", "z", "c"))
    queries, keys, values = queries[0], keys[0], values[0]
    weight = lax.all_gather(out_proj, ("z", "c"), axis=0, tiled=True)
    down = lax.all_gather(w_down[0], "y", axis=0, tiled=True)
    gate_pieces = join_pieces(w_gate[0])
    states = block_states(keys, values)
    states = lax.all_to_all(states, ("x", "y"), 0, 0, tiled=True)
    prefix_low = block_prefixes(states, gate_pieces[1:3])
    meta = jnp.concatenate([routes[0].T.astype(F32), gates[0].T], axis=0)
    meta = held(meta, token_after([prefix_low]))
    prefix_low = lax.all_to_all(prefix_low, ("x", "y"), 0, 0, tiled=True)
    up_pieces = join_pieces(held(w_up[0], token_after([prefix_low])))
    local = local_parts(queries, keys, values)
    select, weights = route_tables(meta, z, c)
    select = [select[i] for i in range(2 * NZ)]
    weights = [weights[i] for i in range(2 * NZ)]
    tables = [
        [jnp.stack([table[2 * k + p] for k in chunk for p in range(2)]) for table in (select, weights)]
        for chunk in CHUNKS
    ]
    residual_sum, normed = project(
        queries, local, prefix_low, attn_gain[None], weight, residual_in[0], ffn_gain[None],
        [t for pair in tables for t in pair] + gate_pieces[3:],
    )
    half = T // 2
    blocks = [normed] + [None] * (NZ - 1)
    arrived, tokens = [], []
    for chunk, (chosen, _) in zip(CHUNKS, tables):
        near = chunk[0]
        up, down_block = blocks[near - 1], blocks[1 - near]
        if near == 3:
            up = blocks[near - 1] = tied(up, tokens[:1])
        blocks[near], blocks[NZ - near] = shift(up, "z", -1), shift(down_block, "z", 1)
        if near == 3:
            blocks[3] = tied(blocks[3], tokens[1:2])
            far = [shift(blocks[3][:half], "z", -1), shift(blocks[5][half:], "z", 1)]
            blocks[4] = jnp.concatenate(far, axis=0)
        pairs = [b for k in chunk for b in (blocks[k], shift(blocks[k], "c", 1))]
        after = [up_pieces[1:3], tokens[:1], up_pieces[3:] + tokens[1:2]][len(arrived)]
        picked, token = pick_rows(chosen, pairs, after)
        tokens.append(token)
        arrived.append(lax.all_to_all(picked, "x", 0, 0, tiled=True))
    pieces = gate_pieces + up_pieces + [down]
    pieces = [pltpu.with_memory_space_constraint(w, pltpu.HBM) for w in pieces]
    at_y = y[None].astype(jnp.int32)
    near, token = experts_apply(at_y, arrived[:2], pieces, tokens[2:])
    far, _ = experts_apply(at_y, arrived[2:], pieces, [token])
    far = lax.all_to_all(far, "x", 0, 0, tiled=True)
    near = lax.all_to_all(tied(near, [far]), "x", 0, 0, tiled=True)
    own, other = {}, {}

    def mix(chunk, rows, first, after):
        own[chunk], theirs = mix_rows(tables[chunk][1], rows, first, after)
        other[chunk] = shift(theirs, "c", 1)

    def pass_on(chunk, places, ring):
        up, down = ring_add(own[chunk], other[chunk], places, ring)
        return [shift(up, "z", 1), shift(down, "z", -1)]

    mix(2, far, 0, [])
    ring = pass_on(2, (1,), [])
    ring = pass_on(2, (0, 2), ring)
    mix(1, near, 2 * len(CHUNKS[0]), ring)
    mix(0, near, 0, ring)
    ring = pass_on(1, (0, 1), ring)
    ring = pass_on(0, (0, 2), ring)
    return final_sum(residual_sum, own[0], other[0], *ring, 1)[None]


def solution(mesh):
    shape = (NX, mesh.devices.shape[0] // NX, mesh.devices.shape[1] // 2, 2)
    grid = Mesh(mesh.devices.reshape(shape), ("x", "y", "z", "c"))
    tm, ep = ("x", "y"), ("z", "c")
    frames = P(ep, tm, None)
    pieces = P(ep + tm, None, None)
    placed = (frames, frames, frames, frames, P(), P(ep, None), P(), pieces, pieces, pieces, frames, frames)
    return jax.shard_map(
        shards, mesh=grid, in_specs=placed, out_specs=frames, check_vma=False
    )
```

```python
import jax
import jax.numpy as jnp
from jax import lax
from jax.experimental import pallas as pl
from jax.experimental.pallas import tpu as pltpu
from jax.sharding import Mesh
from jax.sharding import PartitionSpec as P

HEADS = 16
DH = 128
D = 2048
T = 128
BLK = 32
MOST = 4
NX = 4
NZ = 8
SLOTS = T // BLK * MOST
HID = 256
EPS = 1e-05
MIB = 1 << 20
CHUNKS = ((1, 0, 7), (2, 6), (3, 4, 5))
BF = jnp.bfloat16
F32 = jnp.float32


def dot(a, b, ca=1, cb=0):
    return lax.dot_general(a, b, (((ca,), (cb,)), ((), ())), preferred_element_type=F32)


def shift(value, axis, step):
    count = lax.axis_size(axis)
    return lax.ppermute(value, axis, [(i, (i + step) % count) for i in range(count)])


TILE = 512
ANYWHERE = pl.BlockSpec(memory_space=pl.ANY)
UNREAD = pl.BlockSpec(memory_space=pltpu.HBM)
ON_CHIP = pl.BlockSpec(memory_space=pltpu.VMEM)
TOKEN = jax.ShapeDtypeStruct((8, 128), F32)
TOKEN_SPEC = pl.BlockSpec((8, 128), lambda j: (0, 0))


def column_tile(rows):
    return pl.BlockSpec((rows, TILE), lambda j: (0, j))


def state_kernel(k_ref, v_ref, state_ref):
    for h in range(HEADS):
        at = slice(h * DH, (h + 1) * DH)
        state_ref[h] = dot(k_ref[:, at], v_ref[:, at], 0, 0)


def block_states(keys, values):
    return pl.pallas_call(
        state_kernel,
        out_shape=jax.ShapeDtypeStruct((HEADS, DH, DH), F32),
        name="block_states",
    )(keys, values)


def prefix_kernel(state_ref, out_ref):
    running = jnp.zeros((DH, DH), F32)
    for i in range(HEADS):
        out_ref[i] = running.astype(BF)
        running = running + state_ref[i]


def corner(value):
    return lax.slice(value, (0,) * value.ndim, (1,) * (value.ndim - 2) + (16, 128))


def untouched(kernel, count):
    return lambda *refs: kernel(*refs[count:])


def block_prefixes(states, after):
    after = [corner(v) if v.size > 1024 else v for v in after]
    return pl.pallas_call(
        untouched(prefix_kernel, len(after)),
        in_specs=[UNREAD] * len(after) + [pl.BlockSpec(memory_space=pltpu.VMEM)],
        out_shape=jax.ShapeDtypeStruct(states.shape, BF),
        name="block_prefixes",
    )(*after, states)


def token_kernel(*refs):
    refs[-1][...] = jnp.zeros_like(refs[-1])


def token_after(after):
    after = [corner(v) for v in after]
    return pl.pallas_call(
        token_kernel,
        in_specs=[UNREAD] * len(after),
        out_shape=TOKEN,
        name="token_after",
    )(*after)


def held(value, token):
    return jnp.where(token[0, 0] == 0.0, value, jnp.zeros_like(value))


def tied(value, after):
    after = [corner(v) if v.size > 1024 else v for v in after]
    return pl.pallas_call(
        lambda *refs: None,
        in_specs=[ANYWHERE] + [UNREAD] * len(after),
        out_specs=ANYWHERE,
        out_shape=jax.ShapeDtypeStruct(value.shape, value.dtype),
        input_output_aliases={0: 0},
        name="tied",
    )(value, *after)


def local_kernel(q_ref, k_ref, v_ref, out_ref):
    rows = lax.broadcasted_iota(jnp.int32, (T, T), 0)
    columns = lax.broadcasted_iota(jnp.int32, (T, T), 1)
    for h in range(4):
        at = slice(h * DH, (h + 1) * DH)
        scores = dot(q_ref[:, at], k_ref[:, at], 1, 1)
        scores = jnp.where(rows >= columns, scores, 0.0).astype(BF)
        out_ref[:, at] = dot(scores, v_ref[:, at])


def local_parts(queries, keys, values):
    heads = pl.BlockSpec((T, 4 * DH), lambda h: (0, h))
    return pl.pallas_call(
        local_kernel,
        grid=(HEADS // 4,),
        in_specs=[heads] * 3,
        out_specs=heads,
        out_shape=jax.ShapeDtypeStruct((T, D), F32),
        name="local_parts",
    )(queries, keys, values)


def project_kernel(
    q_ref, local_ref, prefix_ref, gain_ref, w_ref, res_ref, fgain_ref, sum_ref, normed_ref, att, acc
):
    step = pl.program_id(0)

    @pl.when(step == 0)
    def _():
        for h in range(HEADS):
            at = slice(h * DH, (h + 1) * DH)
            mixed = local_ref[:, at] + dot(q_ref[:, at], prefix_ref[h])
            scale = lax.rsqrt(jnp.mean(mixed * mixed, axis=-1, keepdims=True) + EPS)
            att[:, at] = (mixed * scale * gain_ref[:, at]).astype(BF)

    acc[step] = res_ref[...].astype(F32) + dot(att[...], w_ref[...])

    @pl.when(step == D // TILE - 1)
    def _():
        total = jnp.concatenate([acc[i] for i in range(D // TILE)], axis=1)
        norm = lax.rsqrt(jnp.mean(total * total, axis=-1, keepdims=True) + EPS)
        sum_ref[...] = total
        normed_ref[...] = (total * norm * fgain_ref[...]).astype(BF)


def project(queries, local, prefix_low, attn_gain, weight, residual, ffn_gain, after):
    after = [corner(v) if v.size > 1024 else v for v in after]
    whole = pl.BlockSpec((T, D), lambda j: (0, 0))
    row = pl.BlockSpec((1, D), lambda j: (0, 0))
    weight = pltpu.with_memory_space_constraint(weight, pltpu.HBM)
    return pl.pallas_call(
        untouched(project_kernel, len(after)),
        grid=(D // TILE,),
        in_specs=[UNREAD] * len(after)
        + [
            whole,
            whole,
            pl.BlockSpec((HEADS, DH, DH), lambda j: (0, 0, 0)),
            row,
            column_tile(D),
            column_tile(T),
            row,
        ],
        out_specs=[whole, whole],
        out_shape=[jax.ShapeDtypeStruct((T, D), F32), jax.ShapeDtypeStruct((T, D), BF)],
        scratch_shapes=[pltpu.VMEM((T, D), BF), pltpu.VMEM((D // TILE, T, TILE), F32)],
        compiler_params=pltpu.CompilerParams(vmem_limit_bytes=20 * MIB),
        name="project",
    )(*after, queries, local, prefix_low, attn_gain, weight, residual, ffn_gain)


def route_tables(meta, z, c):
    meta = jnp.stack([meta, shift(meta, "c", 1)])[None]
    for step in (1, 2, 4):
        meta = jnp.concatenate([meta, shift(meta, "z", -step)], axis=0)
    meta = jnp.concatenate([meta[k : k + 1] for chunk in CHUNKS for k in chunk], axis=0)
    meta = meta.reshape(2 * NZ, 8, T)
    picks, gains = meta[:, :MOST], meta[:, MOST:]
    offsets = jnp.arange(NX, dtype=jnp.int32)
    experts = ((2 * z + c) * NX + offsets).astype(F32)
    hit = picks[:, None, :, :] == experts[None, :, None, None]
    named = jnp.any(hit, axis=2)
    gain = jnp.sum(jnp.where(hit, gains[:, None], 0.0), axis=2)
    frame = jnp.arange(T, dtype=jnp.int32)
    earlier = (frame[:, None] < frame[None, :]) & (frame[:, None] // BLK == frame[None, :] // BLK)
    rank = lax.dot_general(
        named.astype(BF), earlier.astype(BF), (((2,), (0,)), ((), ())), preferred_element_type=F32
    )
    slot = rank.astype(jnp.int32) + frame // BLK * MOST
    taken = named & (rank < MOST)
    match = taken[:, :, None, :] & (
        slot[:, :, None, :] == jnp.arange(SLOTS, dtype=jnp.int32)[None, None, :, None]
    )
    select = match.astype(BF).reshape(2 * NZ, NX * SLOTS, T)
    high = lax.reduce_precision(gain, 8, 7)
    low = gain - high
    split = [
        jnp.where(match, part[:, :, None, :], 0.0).astype(BF).reshape(2 * NZ, NX * SLOTS, T)
        for part in (high, low)
    ]
    return select, jnp.concatenate(split, axis=1)


def pick_kernel(count, first, s_ref, *refs):
    out, token = refs[count:]
    token[...] = jnp.zeros_like(token)
    for i in range(count):
        rows = dot(s_ref[first + i], refs[i][...]).astype(BF)
        for j in range(NX):
            out[j, pl.ds(i * SLOTS, SLOTS), :] = rows[j * SLOTS : (j + 1) * SLOTS]


def pick_rows(select, first, blocks, after):
    count = len(blocks)
    after = [corner(v) if v.size > 1024 else v for v in after]
    return pl.pallas_call(
        untouched(lambda *refs: pick_kernel(count, first, *refs), len(after)),
        in_specs=[UNREAD] * len(after) + [ON_CHIP] * (1 + count),
        out_specs=[ON_CHIP] * 2,
        out_shape=[jax.ShapeDtypeStruct((NX, count * SLOTS, D), BF), TOKEN],
        name="pick_rows",
    )(*after, select, *blocks)


def mix_kernel(count, first, t_ref, rows_ref, own_ref, other_ref):
    for i in range(count):
        at = pl.ds(i * SLOTS, SLOTS)
        out = other_ref if i % 2 else own_ref
        for j in range(0, D, TILE):
            rows = jnp.concatenate([rows_ref[e, at, j : j + TILE] for e in range(NX)] * 2, axis=0)
            out[pl.ds(i // 2 * T, T), j : j + TILE] = dot(t_ref[first + i], rows, 0, 0).astype(BF)


def mix_rows(weights, first, rows, after):
    count = rows.shape[1] // SLOTS
    after = [corner(v) if v.size > 1024 else v for v in after]
    return pl.pallas_call(
        untouched(lambda *refs: mix_kernel(count, first, *refs), len(after)),
        in_specs=[UNREAD] * len(after) + [ON_CHIP] * 2,
        out_specs=[ON_CHIP] * 2,
        out_shape=[jax.ShapeDtypeStruct((count // 2 * T, D), BF)] * 2,
        name="mix_rows",
    )(*after, weights, rows)


def expert_kernel(sizes, at_y, *refs):
    n_in = len(sizes)
    inputs, weights = refs[:n_in], refs[n_in : n_in + 11]
    outs, token = refs[n_in + 11 : 2 * n_in + 11], refs[2 * n_in + 11]
    x_buf, g_buf, u_buf, d_buf, h_buf, o_buf, x_sem, g_sem, u_sem, d_sem, o_sem = refs[2 * n_in + 12 :]
    token[...] = jnp.zeros_like(token)
    starts = [sum(sizes[:i]) for i in range(n_in)]
    rows = sum(sizes)
    half = D // 2
    targets = [(0, 0, D), (1, 0, D), (2, 0, D), (3, 0, half), (3, half, half)]
    x_copies = [
        pltpu.make_async_copy(inputs[i], x_buf.at[pl.ds(starts[i], sizes[i])], x_sem.at[i])
        for i in range(n_in)
    ]

    def up_copies(first_ref, buf, sem):
        return [
            pltpu.make_async_copy(weights[first_ref + i], buf.at[g, pl.ds(first, size)], sem.at[i])
            for i, (g, first, size) in enumerate(targets)
        ]

    g_copies, u_copies = up_copies(0, g_buf, g_sem), up_copies(5, u_buf, u_sem)
    d_copies = []
    for i, offset in enumerate((0, 3, 1, 2)):
        source = pl.multiple_of(lax.rem(at_y[0] + offset, 4) * HID, HID)
        d_copies.append(
            pltpu.make_async_copy(
                weights[10].at[pl.ds(source, HID)], d_buf.at[pl.ds(i * HID, HID)], d_sem.at[i]
            )
        )
    for copy in x_copies:
        copy.start()
    for i in range(5):
        g_copies[i].start()
        u_copies[i].start()
    for copy in d_copies:
        copy.start()
    for copy in x_copies:
        copy.wait()
    for g in range(4):
        for i in ([g], [3, 4])[g == 3]:
            g_copies[i].wait()
            u_copies[i].wait()
        gate = dot(x_buf[...], g_buf[g])
        up = dot(x_buf[...], u_buf[g])
        h_buf[:, g * HID : (g + 1) * HID] = (gate / (1.0 + jnp.exp(-gate)) * up).astype(BF)
    for copy in d_copies:
        copy.wait()

    def out_columns(j, _):
        at = pl.ds(pl.multiple_of(j * TILE, TILE), TILE)
        o_buf[:, at] = dot(h_buf[...], d_buf[:, at]).astype(BF)
        return 0

    lax.fori_loop(0, D // TILE, out_columns, 0)
    o_copies = []
    for i in range(n_in):
        copy = pltpu.make_async_copy(o_buf.at[pl.ds(starts[i], sizes[i])], outs[i], o_sem.at[i])
        copy.start()
        o_copies.append(copy)
    for copy in o_copies:
        copy.wait()


def experts_apply(at_y, chunks, weights, after):
    after = [corner(v) if v.size > 1024 else v for v in after]
    buffers = [chunk.reshape(-1, D) for chunk in chunks]
    sizes = tuple(b.shape[0] for b in buffers)
    rows = sum(sizes)
    *outs, token = pl.pallas_call(
        untouched(lambda *refs: expert_kernel(sizes, *refs), len(after)),
        in_specs=[UNREAD] * len(after)
        + [pl.BlockSpec(memory_space=pltpu.SMEM)]
        + [ANYWHERE] * len(sizes)
        + [UNREAD] * 11,
        out_specs=[ANYWHERE] * len(sizes) + [ON_CHIP],
        out_shape=[jax.ShapeDtypeStruct((n, D), BF) for n in sizes] + [TOKEN],
        scratch_shapes=[
            pltpu.VMEM((rows, D), BF),
            pltpu.VMEM((4, D, HID), BF),
            pltpu.VMEM((4, D, HID), BF),
            pltpu.VMEM((4 * HID, D), BF),
            pltpu.VMEM((rows, 4 * HID), BF),
            pltpu.VMEM((rows, D), BF),
            pltpu.SemaphoreType.DMA((len(sizes),)),
            pltpu.SemaphoreType.DMA((5,)),
            pltpu.SemaphoreType.DMA((5,)),
            pltpu.SemaphoreType.DMA((4,)),
            pltpu.SemaphoreType.DMA((len(sizes),)),
        ],
        compiler_params=pltpu.CompilerParams(vmem_limit_bytes=26 * MIB),
        name="experts",
    )(*after, at_y, *buffers, *weights)
    return [out.reshape(chunk.shape) for out, chunk in zip(outs, chunks)], token


def join_pieces(piece):
    half = piece.shape[0] // 2
    below, above = shift(piece, "y", 1), shift(piece, "y", -1)
    far_first = shift(below[:half], "y", 1)
    far_second = shift(above[half:], "y", -1)
    return [piece, below, above, far_first, far_second]


def ring_add(own, other, places, ring):
    half = T // 2
    up, down = (
        own[p * T : (p + 1) * T].astype(F32) + other[p * T : (p + 1) * T].astype(F32)
        for p in (places[0], places[-1])
    )
    if not ring:
        return up[:half].astype(BF), down[half:].astype(BF)
    first, second = (r.astype(F32) for r in lax.optimization_barrier(tuple(ring)))
    if first.shape[0] == half:
        first = jnp.concatenate([first, jnp.zeros_like(first)], axis=0)
        second = jnp.concatenate([jnp.zeros_like(second), second], axis=0)
    return (up + first).astype(BF), (down + second).astype(BF)


def final_sum(residual_sum, own, other, up, down, place):
    at = slice(place * T, (place + 1) * T)
    mixture = own[at].astype(F32) + other[at].astype(F32) + up.astype(F32) + down.astype(F32)
    return (residual_sum + mixture).astype(BF)


def shards(
    queries, keys, values, residual_in, attn_gain, out_proj, ffn_gain,
    w_gate, w_up, w_down, routes, gates,
):
    y, z, c = (lax.axis_index(name) for name in ("y", "z", "c"))
    queries, keys, values = queries[0], keys[0], values[0]
    weight = lax.all_gather(out_proj, ("z", "c"), axis=0, tiled=True)
    down = lax.all_gather(w_down[0], "y", axis=0, tiled=True)
    gate_pieces = join_pieces(w_gate[0])
    states = block_states(keys, values)
    states = lax.all_to_all(states, ("x", "y"), 0, 0, tiled=True)
    prefix_low = block_prefixes(states, [])
    up_pieces = join_pieces(held(w_up[0], token_after([prefix_low] + gate_pieces[1:3])))
    prefix_low = lax.all_to_all(prefix_low, ("x", "y"), 0, 0, tiled=True)
    token = token_after([prefix_low])
    meta = jnp.concatenate([routes[0].T.astype(F32), gates[0].T], axis=0)
    local = local_parts(queries, keys, values)
    select, weights = route_tables(held(meta, token), z, c)
    residual_sum, normed = project(
        queries, local, prefix_low, attn_gain[None], weight, residual_in[0], ffn_gain[None],
        [select, weights] + gate_pieces[3:] + up_pieces[1:3],
    )
    half = T // 2
    blocks = [normed] + [None] * (NZ - 1)
    arrived, tokens = [], []
    firsts = [2 * sum(len(chunk) for chunk in CHUNKS[:i]) for i in range(len(CHUNKS))]
    for chunk, first in zip(CHUNKS, firsts):
        near = chunk[0]
        up, down_block = blocks[near - 1], blocks[1 - near]
        if near == 3:
            up = blocks[near - 1] = tied(up, tokens[:1])
        blocks[near], blocks[NZ - near] = shift(up, "z", -1), shift(down_block, "z", 1)
        if near == 3:
            blocks[3] = tied(blocks[3], tokens[1:2])
            far = [shift(blocks[3][:half], "z", -1), shift(blocks[5][half:], "z", 1)]
            blocks[4] = jnp.concatenate(far, axis=0)
        pairs = [b for k in chunk for b in (blocks[k], shift(blocks[k], "c", 1))]
        picked, token = pick_rows(select, first, pairs, tokens)
        tokens.append(token)
        arrived.append(lax.all_to_all(picked, "x", 0, 0, tiled=True))
    pieces = gate_pieces + up_pieces + [down]
    pieces = [pltpu.with_memory_space_constraint(w, pltpu.HBM) for w in pieces]
    at_y = y[None].astype(jnp.int32)
    near, token = experts_apply(at_y, arrived[:2], pieces, tokens[2:])
    (far,), _ = experts_apply(at_y, arrived[2:], pieces, [token])
    returned = [None] * 3
    returned[1] = lax.all_to_all(tied(near[1], [corner(arrived[2])]), "x", 0, 0, tiled=True)
    returned[2] = lax.all_to_all(tied(far, [corner(returned[1])]), "x", 0, 0, tiled=True)
    returned[0] = lax.all_to_all(tied(near[0], [corner(returned[2])]), "x", 0, 0, tiled=True)
    own, other = {}, {}

    def mix(chunk, after):
        own[chunk], theirs = mix_rows(weights, firsts[chunk], returned[chunk], after)
        other[chunk] = shift(theirs, "c", 1)

    def pass_on(chunk, places, ring):
        up, down = ring_add(own[chunk], other[chunk], places, ring)
        return [shift(up, "z", 1), shift(down, "z", -1)]

    mix(1, [])
    mix(2, [])
    ring = pass_on(2, (1,), [])
    ring = pass_on(2, (0, 2), ring)
    mix(0, ring)
    ring = pass_on(1, (0, 1), ring)
    ring = pass_on(0, (0, 2), ring)
    return final_sum(residual_sum, own[0], other[0], *ring, 1)[None]


def solution(mesh):
    shape = (NX, mesh.devices.shape[0] // NX, mesh.devices.shape[1] // 2, 2)
    grid = Mesh(mesh.devices.reshape(shape), ("x", "y", "z", "c"))
    tm, ep = ("x", "y"), ("z", "c")
    frames = P(ep, tm, None)
    pieces = P(ep + tm, None, None)
    placed = (frames, frames, frames, frames, P(), P(ep, None), P(), pieces, pieces, pieces, frames, frames)
    return jax.shard_map(
        shards, mesh=grid, in_specs=placed, out_specs=frames, check_vma=False
    )
```

```python
import jax
import jax.numpy as jnp
from jax import lax
from jax.experimental import pallas as pl
from jax.experimental.pallas import tpu as pltpu
from jax.sharding import Mesh
from jax.sharding import PartitionSpec as P

HEADS = 16
DH = 128
D = 2048
T = 128
BLK = 32
MOST = 4
NX = 4
NZ = 8
SLOTS = T // BLK * MOST
HID = 256
EPS = 1e-05
MIB = 1 << 20
CHUNKS = ((1, 0, 7), (2, 6), (3, 4, 5))
BF = jnp.bfloat16
F32 = jnp.float32


def dot(a, b, ca=1, cb=0):
    return lax.dot_general(a, b, (((ca,), (cb,)), ((), ())), preferred_element_type=F32)


def shift(value, axis, step):
    count = lax.axis_size(axis)
    return lax.ppermute(value, axis, [(i, (i + step) % count) for i in range(count)])


TILE = 512
ANYWHERE = pl.BlockSpec(memory_space=pl.ANY)
UNREAD = pl.BlockSpec(memory_space=pltpu.HBM)
ON_CHIP = pl.BlockSpec(memory_space=pltpu.VMEM)
TOKEN = jax.ShapeDtypeStruct((8, 128), F32)
TOKEN_SPEC = pl.BlockSpec((8, 128), lambda j: (0, 0))


def column_tile(rows):
    return pl.BlockSpec((rows, TILE), lambda j: (0, j))


def state_kernel(k_ref, v_ref, state_ref):
    for h in range(HEADS):
        at = slice(h * DH, (h + 1) * DH)
        state_ref[h] = dot(k_ref[:, at], v_ref[:, at], 0, 0)


def block_states(keys, values):
    return pl.pallas_call(
        state_kernel,
        out_shape=jax.ShapeDtypeStruct((HEADS, DH, DH), F32),
        name="block_states",
    )(keys, values)


def prefix_kernel(state_ref, out_ref):
    running = jnp.zeros((DH, DH), F32)
    for i in range(HEADS):
        out_ref[i] = running.astype(BF)
        running = running + state_ref[i]


def corner(value):
    return lax.slice(value, (0,) * value.ndim, (1,) * (value.ndim - 2) + (16, 128))


def untouched(kernel, count):
    return lambda *refs: kernel(*refs[count:])


def block_prefixes(states, after):
    after = [corner(v) if v.size > 1024 else v for v in after]
    return pl.pallas_call(
        untouched(prefix_kernel, len(after)),
        in_specs=[UNREAD] * len(after) + [pl.BlockSpec(memory_space=pltpu.VMEM)],
        out_shape=jax.ShapeDtypeStruct(states.shape, BF),
        name="block_prefixes",
    )(*after, states)


def token_kernel(*refs):
    refs[-1][...] = jnp.zeros_like(refs[-1])


def token_after(after):
    after = [corner(v) for v in after]
    return pl.pallas_call(
        token_kernel,
        in_specs=[UNREAD] * len(after),
        out_shape=TOKEN,
        name="token_after",
    )(*after)


def held(value, token):
    return jnp.where(token[0, 0] == 0.0, value, jnp.zeros_like(value))


def tied(value, after):
    after = [corner(v) if v.size > 1024 else v for v in after]
    return pl.pallas_call(
        lambda *refs: None,
        in_specs=[ANYWHERE] + [UNREAD] * len(after),
        out_specs=ANYWHERE,
        out_shape=jax.ShapeDtypeStruct(value.shape, value.dtype),
        input_output_aliases={0: 0},
        name="tied",
    )(value, *after)


def local_kernel(q_ref, k_ref, v_ref, out_ref):
    rows = lax.broadcasted_iota(jnp.int32, (T, T), 0)
    columns = lax.broadcasted_iota(jnp.int32, (T, T), 1)
    for h in range(4):
        at = slice(h * DH, (h + 1) * DH)
        scores = dot(q_ref[:, at], k_ref[:, at], 1, 1)
        scores = jnp.where(rows >= columns, scores, 0.0).astype(BF)
        out_ref[:, at] = dot(scores, v_ref[:, at])


def local_parts(queries, keys, values):
    heads = pl.BlockSpec((T, 4 * DH), lambda h: (0, h))
    return pl.pallas_call(
        local_kernel,
        grid=(HEADS // 4,),
        in_specs=[heads] * 3,
        out_specs=heads,
        out_shape=jax.ShapeDtypeStruct((T, D), F32),
        name="local_parts",
    )(queries, keys, values)


def project_kernel(
    q_ref, local_ref, prefix_ref, gain_ref, w_ref, res_ref, fgain_ref, sum_ref, normed_ref, att, acc
):
    step = pl.program_id(0)

    @pl.when(step == 0)
    def _():
        for h in range(HEADS):
            at = slice(h * DH, (h + 1) * DH)
            mixed = local_ref[:, at] + dot(q_ref[:, at], prefix_ref[h])
            scale = lax.rsqrt(jnp.mean(mixed * mixed, axis=-1, keepdims=True) + EPS)
            att[:, at] = (mixed * scale * gain_ref[:, at]).astype(BF)

    acc[step] = res_ref[...].astype(F32) + dot(att[...], w_ref[...])

    @pl.when(step == D // TILE - 1)
    def _():
        total = jnp.concatenate([acc[i] for i in range(D // TILE)], axis=1)
        norm = lax.rsqrt(jnp.mean(total * total, axis=-1, keepdims=True) + EPS)
        sum_ref[...] = total
        normed_ref[...] = (total * norm * fgain_ref[...]).astype(BF)


def project(queries, local, prefix_low, attn_gain, weight, residual, ffn_gain, after):
    after = [corner(v) if v.size > 1024 else v for v in after]
    whole = pl.BlockSpec((T, D), lambda j: (0, 0))
    row = pl.BlockSpec((1, D), lambda j: (0, 0))
    weight = pltpu.with_memory_space_constraint(weight, pltpu.HBM)
    return pl.pallas_call(
        untouched(project_kernel, len(after)),
        grid=(D // TILE,),
        in_specs=[UNREAD] * len(after)
        + [
            whole,
            whole,
            pl.BlockSpec((HEADS, DH, DH), lambda j: (0, 0, 0)),
            row,
            column_tile(D),
            column_tile(T),
            row,
        ],
        out_specs=[whole, whole],
        out_shape=[jax.ShapeDtypeStruct((T, D), F32), jax.ShapeDtypeStruct((T, D), BF)],
        scratch_shapes=[pltpu.VMEM((T, D), BF), pltpu.VMEM((D // TILE, T, TILE), F32)],
        compiler_params=pltpu.CompilerParams(vmem_limit_bytes=20 * MIB),
        name="project",
    )(*after, queries, local, prefix_low, attn_gain, weight, residual, ffn_gain)


def route_tables(meta, z, c):
    meta = jnp.stack([meta, shift(meta, "c", 1)])[None]
    for step in (1, 2, 4):
        meta = jnp.concatenate([meta, shift(meta, "z", -step)], axis=0)
    meta = jnp.concatenate([meta[k : k + 1] for chunk in CHUNKS for k in chunk], axis=0)
    meta = meta.reshape(2 * NZ, 8, T)
    picks, gains = meta[:, :MOST], meta[:, MOST:]
    offsets = jnp.arange(NX, dtype=jnp.int32)
    experts = ((2 * z + c) * NX + offsets).astype(F32)
    hit = picks[:, None, :, :] == experts[None, :, None, None]
    named = jnp.any(hit, axis=2)
    gain = jnp.sum(jnp.where(hit, gains[:, None], 0.0), axis=2)
    frame = jnp.arange(T, dtype=jnp.int32)
    earlier = (frame[:, None] < frame[None, :]) & (frame[:, None] // BLK == frame[None, :] // BLK)
    rank = lax.dot_general(
        named.astype(BF), earlier.astype(BF), (((2,), (0,)), ((), ())), preferred_element_type=F32
    )
    slot = rank.astype(jnp.int32) + frame // BLK * MOST
    taken = named & (rank < MOST)
    match = taken[:, :, None, :] & (
        slot[:, :, None, :] == jnp.arange(SLOTS, dtype=jnp.int32)[None, None, :, None]
    )
    select = match.astype(BF).reshape(2 * NZ, NX * SLOTS, T)
    high = lax.reduce_precision(gain, 8, 7)
    low = gain - high
    split = [
        jnp.where(match, part[:, :, None, :], 0.0).astype(BF).reshape(2 * NZ, NX * SLOTS, T)
        for part in (high, low)
    ]
    return select, jnp.concatenate(split, axis=1)


def pick_kernel(count, first, s_ref, *refs):
    out, token = refs[count:]
    token[...] = jnp.zeros_like(token)
    for i in range(count):
        rows = dot(s_ref[first + i], refs[i][...]).astype(BF)
        for j in range(NX):
            out[j, pl.ds(i * SLOTS, SLOTS), :] = rows[j * SLOTS : (j + 1) * SLOTS]


def pick_rows(select, first, blocks, after):
    count = len(blocks)
    after = [corner(v) if v.size > 1024 else v for v in after]
    return pl.pallas_call(
        untouched(lambda *refs: pick_kernel(count, first, *refs), len(after)),
        in_specs=[UNREAD] * len(after) + [ON_CHIP] * (1 + count),
        out_specs=[ON_CHIP] * 2,
        out_shape=[jax.ShapeDtypeStruct((NX, count * SLOTS, D), BF), TOKEN],
        name="pick_rows",
    )(*after, select, *blocks)


def mix_kernel(count, first, t_ref, rows_ref, own_ref, other_ref):
    for i in range(count):
        at = pl.ds(i * SLOTS, SLOTS)
        out = other_ref if i % 2 else own_ref
        for j in range(0, D, TILE):
            rows = jnp.concatenate([rows_ref[e, at, j : j + TILE] for e in range(NX)] * 2, axis=0)
            out[pl.ds(i // 2 * T, T), j : j + TILE] = dot(t_ref[first + i], rows, 0, 0).astype(BF)


def mix_rows(weights, first, rows, after):
    count = rows.shape[1] // SLOTS
    after = [corner(v) if v.size > 1024 else v for v in after]
    return pl.pallas_call(
        untouched(lambda *refs: mix_kernel(count, first, *refs), len(after)),
        in_specs=[UNREAD] * len(after) + [ON_CHIP] * 2,
        out_specs=[ON_CHIP] * 2,
        out_shape=[jax.ShapeDtypeStruct((count // 2 * T, D), BF)] * 2,
        name="mix_rows",
    )(*after, weights, rows)


def expert_kernel(sizes, at_y, *refs):
    n_in = len(sizes)
    inputs, weights = refs[:n_in], refs[n_in : n_in + 6]
    outs, token = refs[n_in + 6 : 2 * n_in + 6], refs[2 * n_in + 6]
    x_buf, g_buf, u_buf, d_buf, h_buf, o_buf, x_sem, g_sem, u_sem, d_sem, o_sem = refs[2 * n_in + 7 :]
    token[...] = jnp.zeros_like(token)
    starts = [sum(sizes[:i]) for i in range(n_in)]
    rows = sum(sizes)
    half = D // 2
    targets = [(0, 0, D), (1, 0, D), (2, 0, D), (3, 0, half), (3, half, half)]
    x_copies = [
        pltpu.make_async_copy(inputs[i], x_buf.at[pl.ds(starts[i], sizes[i])], x_sem.at[i])
        for i in range(n_in)
    ]
    g_copies = [
        pltpu.make_async_copy(weights[i], g_buf.at[g, pl.ds(first, size)], g_sem.at[i])
        for i, (g, first, size) in enumerate(targets)
    ]
    u_copies, d_copies = [], []
    for i, offset in enumerate((0, 3, 1, 2)):
        piece = weights[5].at[lax.rem(at_y[0] + offset, 4)]
        u_copies.append(pltpu.make_async_copy(piece.at[pl.ds(0, D)], u_buf.at[i], u_sem.at[i]))
        for j in range(D // HID):
            d_copies.append(
                pltpu.make_async_copy(
                    piece.at[pl.ds(D + j * HID, HID)],
                    d_buf.at[pl.ds(i * HID, HID), pl.ds(j * HID, HID)],
                    d_sem.at[i * (D // HID) + j],
                )
            )
    for copy in x_copies:
        copy.start()
    for i in range(4):
        g_copies[i].start()
        if i == 3:
            g_copies[4].start()
        u_copies[i].start()
    for copy in d_copies:
        copy.start()
    for copy in x_copies:
        copy.wait()
    for g in range(4):
        g_copies[g].wait()
        if g == 3:
            g_copies[4].wait()
        u_copies[g].wait()
        gate = dot(x_buf[...], g_buf[g])
        up = dot(x_buf[...], u_buf[g])
        h_buf[:, g * HID : (g + 1) * HID] = (gate / (1.0 + jnp.exp(-gate)) * up).astype(BF)
    for copy in d_copies:
        copy.wait()

    def out_columns(j, _):
        at = pl.ds(pl.multiple_of(j * TILE, TILE), TILE)
        o_buf[:, at] = dot(h_buf[...], d_buf[:, at]).astype(BF)
        return 0

    lax.fori_loop(0, D // TILE, out_columns, 0)
    o_copies = []
    for i in range(n_in):
        copy = pltpu.make_async_copy(o_buf.at[pl.ds(starts[i], sizes[i])], outs[i], o_sem.at[i])
        copy.start()
        o_copies.append(copy)
    for copy in o_copies:
        copy.wait()


def experts_apply(at_y, chunks, weights, after):
    after = [corner(v) if v.size > 1024 else v for v in after]
    buffers = [chunk.reshape(-1, D) for chunk in chunks]
    sizes = tuple(b.shape[0] for b in buffers)
    rows = sum(sizes)
    *outs, token = pl.pallas_call(
        untouched(lambda *refs: expert_kernel(sizes, *refs), len(after)),
        in_specs=[UNREAD] * len(after)
        + [pl.BlockSpec(memory_space=pltpu.SMEM)]
        + [ANYWHERE] * len(sizes)
        + [UNREAD] * 6,
        out_specs=[ANYWHERE] * len(sizes) + [ON_CHIP],
        out_shape=[jax.ShapeDtypeStruct((n, D), BF) for n in sizes] + [TOKEN],
        scratch_shapes=[
            pltpu.VMEM((rows, D), BF),
            pltpu.VMEM((4, D, HID), BF),
            pltpu.VMEM((4, D, HID), BF),
            pltpu.VMEM((4 * HID, D), BF),
            pltpu.VMEM((rows, 4 * HID), BF),
            pltpu.VMEM((rows, D), BF),
            pltpu.SemaphoreType.DMA((len(sizes),)),
            pltpu.SemaphoreType.DMA((5,)),
            pltpu.SemaphoreType.DMA((4,)),
            pltpu.SemaphoreType.DMA((4 * (D // HID),)),
            pltpu.SemaphoreType.DMA((len(sizes),)),
        ],
        compiler_params=pltpu.CompilerParams(vmem_limit_bytes=26 * MIB),
        name="experts",
    )(*after, at_y, *buffers, *weights)
    return [out.reshape(chunk.shape) for out, chunk in zip(outs, chunks)], token


def join_pieces(piece):
    half = piece.shape[0] // 2
    below, above = shift(piece, "y", 1), shift(piece, "y", -1)
    far_first = shift(below[:half], "y", 1)
    far_second = shift(above[half:], "y", -1)
    return [piece, below, above, far_first, far_second]


def ring_add(own, other, places, ring):
    half = T // 2
    up, down = (
        own[p * T : (p + 1) * T].astype(F32) + other[p * T : (p + 1) * T].astype(F32)
        for p in (places[0], places[-1])
    )
    if not ring:
        return up[:half].astype(BF), down[half:].astype(BF)
    first, second = (r.astype(F32) for r in lax.optimization_barrier(tuple(ring)))
    if first.shape[0] == half:
        first = jnp.concatenate([first, jnp.zeros_like(first)], axis=0)
        second = jnp.concatenate([jnp.zeros_like(second), second], axis=0)
    return (up + first).astype(BF), (down + second).astype(BF)


def final_sum(residual_sum, own, other, up, down, place):
    at = slice(place * T, (place + 1) * T)
    mixture = own[at].astype(F32) + other[at].astype(F32) + up.astype(F32) + down.astype(F32)
    return (residual_sum + mixture).astype(BF)


def shards(
    queries, keys, values, residual_in, attn_gain, out_proj, ffn_gain,
    w_gate, w_up, w_down, routes, gates,
):
    y, z, c = (lax.axis_index(name) for name in ("y", "z", "c"))
    queries, keys, values = queries[0], keys[0], values[0]
    weight = lax.all_gather(out_proj, ("z", "c"), axis=0, tiled=True)
    packed = [w_up[0]] + [w_down[0][:, j : j + HID] for j in range(0, D, HID)]
    packed = lax.all_gather(jnp.concatenate(packed, axis=0), "y", axis=0)
    gate_pieces = join_pieces(w_gate[0])
    states = block_states(keys, values)
    states = lax.all_to_all(states, ("x", "y"), 0, 0, tiled=True)
    prefix_low = block_prefixes(states, [])
    prefix_low = lax.all_to_all(prefix_low, ("x", "y"), 0, 0, tiled=True)
    token = token_after([prefix_low])
    meta = jnp.concatenate([routes[0].T.astype(F32), gates[0].T], axis=0)
    local = local_parts(queries, keys, values)
    select, weights = route_tables(held(meta, token), z, c)
    residual_sum, normed = project(
        queries, local, prefix_low, attn_gain[None], weight, residual_in[0], ffn_gain[None],
        [select, weights] + gate_pieces[1:3],
    )
    half = T // 2
    blocks = [normed] + [None] * (NZ - 1)
    arrived, tokens = [], []
    firsts = [2 * sum(len(chunk) for chunk in CHUNKS[:i]) for i in range(len(CHUNKS))]
    for chunk, first in zip(CHUNKS, firsts):
        near = chunk[0]
        up, down_block = blocks[near - 1], blocks[(1 - near) % NZ]
        if near == 3:
            up = blocks[near - 1] = tied(up, tokens[:1])
        blocks[near], blocks[NZ - near] = shift(up, "z", -1), shift(down_block, "z", 1)
        if near == 3:
            blocks[3] = tied(blocks[3], tokens[1:2])
            far = [shift(blocks[3][:half], "z", -1), shift(blocks[5][half:], "z", 1)]
            blocks[4] = jnp.concatenate(far, axis=0)
        pairs = [b for k in chunk for b in (blocks[k], shift(blocks[k], "c", 1))]
        after = tokens + gate_pieces[3:] if near == 3 else tokens
        picked, token = pick_rows(select, first, pairs, after)
        tokens.append(token)
        arrived.append(lax.all_to_all(picked, "x", 0, 0, tiled=True))
    pieces = gate_pieces + [packed]
    pieces = [pltpu.with_memory_space_constraint(w, pltpu.HBM) for w in pieces]
    at_y = y[None].astype(jnp.int32)
    near, token = experts_apply(at_y, arrived[:2], pieces, tokens[2:])
    (far,), _ = experts_apply(at_y, arrived[2:], pieces, [token])
    returned = [None] * 3
    returned[1] = lax.all_to_all(tied(near[1], [corner(arrived[2])]), "x", 0, 0, tiled=True)
    returned[2] = lax.all_to_all(tied(far, [corner(returned[1])]), "x", 0, 0, tiled=True)
    returned[0] = lax.all_to_all(tied(near[0], [corner(returned[2])]), "x", 0, 0, tiled=True)
    own, other = {}, {}

    def mix(chunk, after):
        own[chunk], theirs = mix_rows(weights, firsts[chunk], returned[chunk], after)
        other[chunk] = shift(theirs, "c", 1)

    def pass_on(chunk, places, ring, last=None):
        up, down = ring_add(own[chunk], other[chunk], places, ring)
        if last is not None:
            mix(last, [up])
        return [shift(up, "z", 1), shift(down, "z", -1)]

    mix(1, [])
    mix(2, [own[1]])
    ring = pass_on(2, (1,), [])
    ring = pass_on(2, (0, 2), ring)
    ring = pass_on(1, (0, 1), ring, 0)
    ring = pass_on(0, (0, 2), ring)
    return final_sum(residual_sum, own[0], other[0], *ring, 1)[None]


def solution(mesh):
    shape = (NX, mesh.devices.shape[0] // NX, mesh.devices.shape[1] // 2, 2)
    grid = Mesh(mesh.devices.reshape(shape), ("x", "y", "z", "c"))
    tm, ep = ("x", "y"), ("z", "c")
    frames = P(ep, tm, None)
    pieces = P(ep + tm, None, None)
    placed = (frames, frames, frames, frames, P(), P(ep, None), P(), pieces, pieces, pieces, frames, frames)
    return jax.shard_map(
        shards, mesh=grid, in_specs=placed, out_specs=frames, check_vma=False
    )
```

```python
import jax
import jax.numpy as jnp
from jax import lax
from jax.experimental import pallas as pl
from jax.experimental.pallas import tpu as pltpu
from jax.sharding import Mesh
from jax.sharding import PartitionSpec as P

HEADS = 16
DH = 128
D = 2048
T = 128
BLK = 32
MOST = 4
NX = 4
NZ = 8
SLOTS = T // BLK * MOST
HID = 256
EPS = 1e-05
MIB = 1 << 20
CHUNKS = ((1, 0, 7), (2, 6), (3, 4, 5))
BF = jnp.bfloat16
F32 = jnp.float32


def dot(a, b, ca=1, cb=0):
    return lax.dot_general(a, b, (((ca,), (cb,)), ((), ())), preferred_element_type=F32)


def shift(value, axis, step):
    count = lax.axis_size(axis)
    return lax.ppermute(value, axis, [(i, (i + step) % count) for i in range(count)])


TILE = 512
ANYWHERE = pl.BlockSpec(memory_space=pl.ANY)
UNREAD = pl.BlockSpec(memory_space=pltpu.HBM)
ON_CHIP = pl.BlockSpec(memory_space=pltpu.VMEM)
TOKEN = jax.ShapeDtypeStruct((8, 128), F32)
TOKEN_SPEC = pl.BlockSpec((8, 128), lambda j: (0, 0))


def column_tile(rows):
    return pl.BlockSpec((rows, TILE), lambda j: (0, j))


def state_kernel(k_ref, v_ref, state_ref):
    for h in range(HEADS):
        at = slice(h * DH, (h + 1) * DH)
        state_ref[h] = dot(k_ref[:, at], v_ref[:, at], 0, 0)


def block_states(keys, values):
    return pl.pallas_call(
        state_kernel,
        out_shape=jax.ShapeDtypeStruct((HEADS, DH, DH), F32),
        name="block_states",
    )(keys, values)


def prefix_kernel(state_ref, out_ref):
    running = jnp.zeros((DH, DH), F32)
    for i in range(HEADS):
        out_ref[i] = running.astype(BF)
        running = running + state_ref[i]


def corner(value):
    return lax.slice(value, (0,) * value.ndim, (1,) * (value.ndim - 2) + (16, 128))


def untouched(kernel, count):
    return lambda *refs: kernel(*refs[count:])


def block_prefixes(states, after):
    after = [corner(v) if v.size > 1024 else v for v in after]
    return pl.pallas_call(
        untouched(prefix_kernel, len(after)),
        in_specs=[UNREAD] * len(after) + [pl.BlockSpec(memory_space=pltpu.VMEM)],
        out_shape=jax.ShapeDtypeStruct(states.shape, BF),
        name="block_prefixes",
    )(*after, states)


def token_kernel(*refs):
    refs[-1][...] = jnp.zeros_like(refs[-1])


def token_after(after):
    after = [corner(v) for v in after]
    return pl.pallas_call(
        token_kernel,
        in_specs=[UNREAD] * len(after),
        out_shape=TOKEN,
        name="token_after",
    )(*after)


def held(value, token):
    return jnp.where(token[0, 0] == 0.0, value, jnp.zeros_like(value))


def tied(value, after):
    after = [corner(v) if v.size > 1024 else v for v in after]
    return pl.pallas_call(
        lambda *refs: None,
        in_specs=[ANYWHERE] + [UNREAD] * len(after),
        out_specs=ANYWHERE,
        out_shape=jax.ShapeDtypeStruct(value.shape, value.dtype),
        input_output_aliases={0: 0},
        name="tied",
    )(value, *after)


def local_kernel(q_ref, k_ref, v_ref, out_ref):
    rows = lax.broadcasted_iota(jnp.int32, (T, T), 0)
    columns = lax.broadcasted_iota(jnp.int32, (T, T), 1)
    for h in range(4):
        at = slice(h * DH, (h + 1) * DH)
        scores = dot(q_ref[:, at], k_ref[:, at], 1, 1)
        scores = jnp.where(rows >= columns, scores, 0.0).astype(BF)
        out_ref[:, at] = dot(scores, v_ref[:, at])


def local_parts(queries, keys, values):
    heads = pl.BlockSpec((T, 4 * DH), lambda h: (0, h))
    return pl.pallas_call(
        local_kernel,
        grid=(HEADS // 4,),
        in_specs=[heads] * 3,
        out_specs=heads,
        out_shape=jax.ShapeDtypeStruct((T, D), F32),
        name="local_parts",
    )(queries, keys, values)


def project_kernel(
    q_ref, local_ref, prefix_ref, gain_ref, w_ref, res_ref, fgain_ref, sum_ref, normed_ref, att, acc
):
    step = pl.program_id(0)

    @pl.when(step == 0)
    def _():
        for h in range(HEADS):
            at = slice(h * DH, (h + 1) * DH)
            mixed = local_ref[:, at] + dot(q_ref[:, at], prefix_ref[h])
            scale = lax.rsqrt(jnp.mean(mixed * mixed, axis=-1, keepdims=True) + EPS)
            att[:, at] = (mixed * scale * gain_ref[:, at]).astype(BF)

    acc[step] = res_ref[...].astype(F32) + dot(att[...], w_ref[...])

    @pl.when(step == D // TILE - 1)
    def _():
        total = jnp.concatenate([acc[i] for i in range(D // TILE)], axis=1)
        norm = lax.rsqrt(jnp.mean(total * total, axis=-1, keepdims=True) + EPS)
        sum_ref[...] = total
        normed_ref[...] = (total * norm * fgain_ref[...]).astype(BF)


def project(queries, local, prefix_low, attn_gain, weight, residual, ffn_gain, after):
    after = [corner(v) if v.size > 1024 else v for v in after]
    whole = pl.BlockSpec((T, D), lambda j: (0, 0))
    row = pl.BlockSpec((1, D), lambda j: (0, 0))
    weight = pltpu.with_memory_space_constraint(weight, pltpu.HBM)
    return pl.pallas_call(
        untouched(project_kernel, len(after)),
        grid=(D // TILE,),
        in_specs=[UNREAD] * len(after)
        + [
            whole,
            whole,
            pl.BlockSpec((HEADS, DH, DH), lambda j: (0, 0, 0)),
            row,
            column_tile(D),
            column_tile(T),
            row,
        ],
        out_specs=[whole, whole],
        out_shape=[jax.ShapeDtypeStruct((T, D), F32), jax.ShapeDtypeStruct((T, D), BF)],
        scratch_shapes=[pltpu.VMEM((T, D), BF), pltpu.VMEM((D // TILE, T, TILE), F32)],
        compiler_params=pltpu.CompilerParams(vmem_limit_bytes=20 * MIB),
        name="project",
    )(*after, queries, local, prefix_low, attn_gain, weight, residual, ffn_gain)


def route_tables(meta, z, c):
    meta = jnp.stack([meta, shift(meta, "c", 1)])[None]
    for step in (1, 2, 4):
        meta = jnp.concatenate([meta, shift(meta, "z", -step)], axis=0)
    meta = jnp.concatenate([meta[k : k + 1] for chunk in CHUNKS for k in chunk], axis=0)
    meta = meta.reshape(2 * NZ, 8, T)
    picks, gains = meta[:, :MOST], meta[:, MOST:]
    offsets = jnp.arange(NX, dtype=jnp.int32)
    experts = ((2 * z + c) * NX + offsets).astype(F32)
    hit = picks[:, None, :, :] == experts[None, :, None, None]
    named = jnp.any(hit, axis=2)
    gain = jnp.sum(jnp.where(hit, gains[:, None], 0.0), axis=2)
    frame = jnp.arange(T, dtype=jnp.int32)
    earlier = (frame[:, None] < frame[None, :]) & (frame[:, None] // BLK == frame[None, :] // BLK)
    rank = lax.dot_general(
        named.astype(BF), earlier.astype(BF), (((2,), (0,)), ((), ())), preferred_element_type=F32
    )
    slot = rank.astype(jnp.int32) + frame // BLK * MOST
    taken = named & (rank < MOST)
    match = taken[:, :, None, :] & (
        slot[:, :, None, :] == jnp.arange(SLOTS, dtype=jnp.int32)[None, None, :, None]
    )
    select = match.astype(BF).reshape(2 * NZ, NX * SLOTS, T)
    high = lax.reduce_precision(gain, 8, 7)
    low = gain - high
    split = [
        jnp.where(match, part[:, :, None, :], 0.0).astype(BF).reshape(2 * NZ, NX * SLOTS, T)
        for part in (high, low)
    ]
    return select, jnp.concatenate(split, axis=1)


def pick_kernel(count, first, s_ref, *refs):
    out, token = refs[count:]
    token[...] = jnp.zeros_like(token)
    for i in range(count):
        rows = dot(s_ref[first + i], refs[i][...]).astype(BF)
        for j in range(NX):
            out[j, pl.ds(i * SLOTS, SLOTS), :] = rows[j * SLOTS : (j + 1) * SLOTS]


def pick_rows(select, first, blocks, after):
    count = len(blocks)
    after = [corner(v) if v.size > 1024 else v for v in after]
    return pl.pallas_call(
        untouched(lambda *refs: pick_kernel(count, first, *refs), len(after)),
        in_specs=[UNREAD] * len(after) + [ON_CHIP] * (1 + count),
        out_specs=[ON_CHIP] * 2,
        out_shape=[jax.ShapeDtypeStruct((NX, count * SLOTS, D), BF), TOKEN],
        name="pick_rows",
    )(*after, select, *blocks)


def mix_kernel(count, first, t_ref, rows_ref, own_ref, other_ref):
    for i in range(count):
        at = pl.ds(i * SLOTS, SLOTS)
        out = other_ref if i % 2 else own_ref
        for j in range(0, D, TILE):
            rows = jnp.concatenate([rows_ref[e, at, j : j + TILE] for e in range(NX)] * 2, axis=0)
            out[pl.ds(i // 2 * T, T), j : j + TILE] = dot(t_ref[first + i], rows, 0, 0).astype(BF)


def mix_rows(weights, first, rows, after):
    count = rows.shape[1] // SLOTS
    after = [corner(v) if v.size > 1024 else v for v in after]
    return pl.pallas_call(
        untouched(lambda *refs: mix_kernel(count, first, *refs), len(after)),
        in_specs=[UNREAD] * len(after) + [ON_CHIP] * 2,
        out_specs=[ON_CHIP] * 2,
        out_shape=[jax.ShapeDtypeStruct((count // 2 * T, D), BF)] * 2,
        name="mix_rows",
    )(*after, weights, rows)


def expert_kernel(sizes, at_y, *refs):
    n_in = len(sizes)
    inputs, weights = refs[:n_in], refs[n_in : n_in + 6]
    outs, token = refs[n_in + 6 : 2 * n_in + 6], refs[2 * n_in + 6]
    x_buf, g_buf, u_buf, d_buf, h_buf, o_buf, x_sem, g_sem, u_sem, d_sem, o_sem = refs[2 * n_in + 7 :]
    token[...] = jnp.zeros_like(token)
    starts = [sum(sizes[:i]) for i in range(n_in)]
    rows = sum(sizes)
    half = D // 2
    targets = [(0, 0, D), (1, 0, D), (2, 0, D), (3, 0, half), (3, half, half)]
    x_copies = [
        pltpu.make_async_copy(inputs[i], x_buf.at[pl.ds(starts[i], sizes[i])], x_sem.at[i])
        for i in range(n_in)
    ]
    g_copies = [
        pltpu.make_async_copy(weights[i], g_buf.at[g, pl.ds(first, size)], g_sem.at[i])
        for i, (g, first, size) in enumerate(targets)
    ]
    u_copies, d_copies = [], []
    for i, offset in enumerate((0, 3, 1, 2)):
        piece = weights[5].at[lax.rem(at_y[0] + offset, 4)]
        u_copies.append(pltpu.make_async_copy(piece.at[pl.ds(0, D)], u_buf.at[i], u_sem.at[i]))
        for j in range(D // HID):
            d_copies.append(
                pltpu.make_async_copy(
                    piece.at[pl.ds(D + j * HID, HID)],
                    d_buf.at[pl.ds(i * HID, HID), pl.ds(j * HID, HID)],
                    d_sem.at[i * (D // HID) + j],
                )
            )
    for copy in x_copies:
        copy.start()
    for i in range(4):
        g_copies[i].start()
        if i == 3:
            g_copies[4].start()
        u_copies[i].start()
    for copy in d_copies:
        copy.start()
    for copy in x_copies:
        copy.wait()
    for g in range(4):
        g_copies[g].wait()
        if g == 3:
            g_copies[4].wait()
        u_copies[g].wait()
        gate = dot(x_buf[...], g_buf[g])
        up = dot(x_buf[...], u_buf[g])
        h_buf[:, g * HID : (g + 1) * HID] = (gate / (1.0 + jnp.exp(-gate)) * up).astype(BF)
    for copy in d_copies:
        copy.wait()

    def out_columns(j, _):
        at = pl.ds(pl.multiple_of(j * TILE, TILE), TILE)
        o_buf[:, at] = dot(h_buf[...], d_buf[:, at]).astype(BF)
        return 0

    lax.fori_loop(0, D // TILE, out_columns, 0)
    o_copies = []
    for i in range(n_in):
        copy = pltpu.make_async_copy(o_buf.at[pl.ds(starts[i], sizes[i])], outs[i], o_sem.at[i])
        copy.start()
        o_copies.append(copy)
    for copy in o_copies:
        copy.wait()


def experts_apply(at_y, chunks, weights, after):
    after = [corner(v) if v.size > 1024 else v for v in after]
    buffers = [chunk.reshape(-1, D) for chunk in chunks]
    sizes = tuple(b.shape[0] for b in buffers)
    rows = sum(sizes)
    *outs, token = pl.pallas_call(
        untouched(lambda *refs: expert_kernel(sizes, *refs), len(after)),
        in_specs=[UNREAD] * len(after)
        + [pl.BlockSpec(memory_space=pltpu.SMEM)]
        + [ANYWHERE] * len(sizes)
        + [UNREAD] * 6,
        out_specs=[ANYWHERE] * len(sizes) + [ON_CHIP],
        out_shape=[jax.ShapeDtypeStruct((n, D), BF) for n in sizes] + [TOKEN],
        scratch_shapes=[
            pltpu.VMEM((rows, D), BF),
            pltpu.VMEM((4, D, HID), BF),
            pltpu.VMEM((4, D, HID), BF),
            pltpu.VMEM((4 * HID, D), BF),
            pltpu.VMEM((rows, 4 * HID), BF),
            pltpu.VMEM((rows, D), BF),
            pltpu.SemaphoreType.DMA((len(sizes),)),
            pltpu.SemaphoreType.DMA((5,)),
            pltpu.SemaphoreType.DMA((4,)),
            pltpu.SemaphoreType.DMA((4 * (D // HID),)),
            pltpu.SemaphoreType.DMA((len(sizes),)),
        ],
        compiler_params=pltpu.CompilerParams(vmem_limit_bytes=26 * MIB),
        name="experts",
    )(*after, at_y, *buffers, *weights)
    return [out.reshape(chunk.shape) for out, chunk in zip(outs, chunks)], token


def join_pieces(piece):
    half = piece.shape[0] // 2
    below, above = shift(piece, "y", 1), shift(piece, "y", -1)
    far_first = shift(below[:half], "y", 1)
    far_second = shift(above[half:], "y", -1)
    return [piece, below, above, far_first, far_second]


def ring_add(own, other, places, ring):
    half = T // 2
    up, down = (
        own[p * T : (p + 1) * T].astype(F32) + other[p * T : (p + 1) * T].astype(F32)
        for p in (places[0], places[-1])
    )
    if not ring:
        return up[:half].astype(BF), down[half:].astype(BF)
    first, second = (r.astype(F32) for r in lax.optimization_barrier(tuple(ring)))
    if first.shape[0] == half:
        first = jnp.concatenate([first, jnp.zeros_like(first)], axis=0)
        second = jnp.concatenate([jnp.zeros_like(second), second], axis=0)
    return (up + first).astype(BF), (down + second).astype(BF)


def final_sum(residual_sum, own, other, up, down, place):
    at = slice(place * T, (place + 1) * T)
    mixture = own[at].astype(F32) + other[at].astype(F32) + up.astype(F32) + down.astype(F32)
    return (residual_sum + mixture).astype(BF)


def shards(
    queries, keys, values, residual_in, attn_gain, out_proj, ffn_gain,
    w_gate, w_up, w_down, routes, gates,
):
    y, z, c = (lax.axis_index(name) for name in ("y", "z", "c"))
    queries, keys, values = queries[0], keys[0], values[0]
    weight = lax.all_gather(out_proj, ("z", "c"), axis=0, tiled=True)
    packed = [w_up[0]] + [w_down[0][:, j : j + HID] for j in range(0, D, HID)]
    packed = lax.all_gather(jnp.concatenate(packed, axis=0), "y", axis=0)
    gate_pieces = join_pieces(w_gate[0])
    states = block_states(keys, values)
    token = token_after([states])
    states = lax.all_to_all(states, ("x", "y"), 0, 0, tiled=True)
    prefix_low = block_prefixes(states, [])
    prefix_low = lax.all_to_all(prefix_low, ("x", "y"), 0, 0, tiled=True)
    meta = jnp.concatenate([routes[0].T.astype(F32), gates[0].T], axis=0)
    local = local_parts(queries, keys, values)
    select, weights = route_tables(held(meta, token), z, c)
    residual_sum, normed = project(
        queries, local, prefix_low, attn_gain[None], weight, residual_in[0], ffn_gain[None],
        [select, weights] + gate_pieces[1:3],
    )
    blocks = [normed] + [None] * (NZ - 1)
    arrived, tokens = [], []
    firsts = [2 * sum(len(chunk) for chunk in CHUNKS[:i]) for i in range(len(CHUNKS))]
    for chunk, first in zip(CHUNKS, firsts):
        near = chunk[0]
        up, down_block = blocks[near - 1], blocks[(1 - near) % NZ]
        if near == 3:
            up = blocks[near - 1] = tied(up, tokens[:1])
        blocks[near], blocks[NZ - near] = shift(up, "z", -1), shift(down_block, "z", 1)
        if near == 3:
            blocks[4] = shift(tied(blocks[3], tokens[1:2]), "z", -1)
        pairs = [b for k in chunk for b in (blocks[k], shift(blocks[k], "c", 1))]
        after = tokens + gate_pieces[3:] if near == 2 else tokens
        picked, token = pick_rows(select, first, pairs, after)
        tokens.append(token)
        arrived.append(lax.all_to_all(picked, "x", 0, 0, tiled=True))
    pieces = gate_pieces + [packed]
    pieces = [pltpu.with_memory_space_constraint(w, pltpu.HBM) for w in pieces]
    at_y = y[None].astype(jnp.int32)
    near, token = experts_apply(at_y, arrived[:2], pieces, tokens[2:])
    (far,), _ = experts_apply(at_y, arrived[2:], pieces, [token])
    returned = [None] * 3
    returned[1] = lax.all_to_all(tied(near[1], [corner(arrived[2])]), "x", 0, 0, tiled=True)
    returned[2] = lax.all_to_all(tied(far, [corner(returned[1])]), "x", 0, 0, tiled=True)
    returned[0] = lax.all_to_all(tied(near[0], [corner(returned[2])]), "x", 0, 0, tiled=True)
    own, other = {}, {}

    def mix(chunk, after):
        own[chunk], theirs = mix_rows(weights, firsts[chunk], returned[chunk], after)
        other[chunk] = shift(theirs, "c", 1)

    def pass_on(chunk, places, ring, last=None):
        up, down = ring_add(own[chunk], other[chunk], places, ring)
        if last is not None:
            mix(last, [up])
        return [shift(up, "z", 1), shift(down, "z", -1)]

    mix(1, [])
    mix(2, [own[1]])
    ring = pass_on(2, (1,), [])
    ring = pass_on(2, (0, 2), ring)
    ring = pass_on(1, (0, 1), ring, 0)
    ring = pass_on(0, (0, 2), ring)
    return final_sum(residual_sum, own[0], other[0], *ring, 1)[None]


def solution(mesh):
    shape = (NX, mesh.devices.shape[0] // NX, mesh.devices.shape[1] // 2, 2)
    grid = Mesh(mesh.devices.reshape(shape), ("x", "y", "z", "c"))
    tm, ep = ("x", "y"), ("z", "c")
    frames = P(ep, tm, None)
    pieces = P(ep + tm, None, None)
    placed = (frames, frames, frames, frames, P(), P(ep, None), P(), pieces, pieces, pieces, frames, frames)
    return jax.shard_map(
        shards, mesh=grid, in_specs=placed, out_specs=frames, check_vma=False
    )
```

```python
import jax
import jax.numpy as jnp
from jax import lax
from jax.experimental import pallas as pl
from jax.experimental.pallas import tpu as pltpu
from jax.sharding import Mesh
from jax.sharding import PartitionSpec as P

HEADS = 16
DH = 128
D = 2048
T = 128
BLK = 32
MOST = 4
NX = 4
NZ = 8
SLOTS = T // BLK * MOST
HID = 256
EPS = 1e-05
MIB = 1 << 20
CHUNKS = ((1, 0, 7), (2, 6), (3, 4, 5))
BF = jnp.bfloat16
F32 = jnp.float32


def dot(a, b, ca=1, cb=0):
    return lax.dot_general(a, b, (((ca,), (cb,)), ((), ())), preferred_element_type=F32)


def shift(value, axis, step):
    count = lax.axis_size(axis)
    return lax.ppermute(value, axis, [(i, (i + step) % count) for i in range(count)])


TILE = 512
ANYWHERE = pl.BlockSpec(memory_space=pl.ANY)
UNREAD = pl.BlockSpec(memory_space=pltpu.HBM)
ON_CHIP = pl.BlockSpec(memory_space=pltpu.VMEM)
TOKEN = jax.ShapeDtypeStruct((8, 128), F32)
TOKEN_SPEC = pl.BlockSpec((8, 128), lambda j: (0, 0))


def column_tile(rows):
    return pl.BlockSpec((rows, TILE), lambda j: (0, j))


def state_kernel(k_ref, v_ref, state_ref):
    for h in range(HEADS):
        at = slice(h * DH, (h + 1) * DH)
        state_ref[h] = dot(k_ref[:, at], v_ref[:, at], 0, 0)


def block_states(keys, values):
    return pl.pallas_call(
        state_kernel,
        out_shape=jax.ShapeDtypeStruct((HEADS, DH, DH), F32),
        name="block_states",
    )(keys, values)


def prefix_kernel(state_ref, out_ref):
    running = jnp.zeros((DH, DH), F32)
    for i in range(HEADS):
        out_ref[i] = running.astype(BF)
        running = running + state_ref[i]


def corner(value):
    return lax.slice(value, (0,) * value.ndim, (1,) * (value.ndim - 2) + (16, 128))


def untouched(kernel, count):
    return lambda *refs: kernel(*refs[count:])


def block_prefixes(states, after):
    after = [corner(v) if v.size > 1024 else v for v in after]
    return pl.pallas_call(
        untouched(prefix_kernel, len(after)),
        in_specs=[UNREAD] * len(after) + [pl.BlockSpec(memory_space=pltpu.VMEM)],
        out_shape=jax.ShapeDtypeStruct(states.shape, BF),
        name="block_prefixes",
    )(*after, states)


def token_kernel(*refs):
    refs[-1][...] = jnp.zeros_like(refs[-1])


def token_after(after):
    after = [corner(v) for v in after]
    return pl.pallas_call(
        token_kernel,
        in_specs=[UNREAD] * len(after),
        out_shape=TOKEN,
        name="token_after",
    )(*after)


def held(value, token):
    return jnp.where(token[0, 0] == 0.0, value, jnp.zeros_like(value))


def tied(value, after):
    after = [corner(v) if v.size > 1024 else v for v in after]
    return pl.pallas_call(
        lambda *refs: None,
        in_specs=[ANYWHERE] + [UNREAD] * len(after),
        out_specs=ANYWHERE,
        out_shape=jax.ShapeDtypeStruct(value.shape, value.dtype),
        input_output_aliases={0: 0},
        name="tied",
    )(value, *after)


def local_kernel(q_ref, k_ref, v_ref, out_ref):
    rows = lax.broadcasted_iota(jnp.int32, (T, T), 0)
    columns = lax.broadcasted_iota(jnp.int32, (T, T), 1)
    for h in range(4):
        at = slice(h * DH, (h + 1) * DH)
        scores = dot(q_ref[:, at], k_ref[:, at], 1, 1)
        scores = jnp.where(rows >= columns, scores, 0.0).astype(BF)
        out_ref[:, at] = dot(scores, v_ref[:, at])


def local_parts(queries, keys, values):
    heads = pl.BlockSpec((T, 4 * DH), lambda h: (0, h))
    return pl.pallas_call(
        local_kernel,
        grid=(HEADS // 4,),
        in_specs=[heads] * 3,
        out_specs=heads,
        out_shape=jax.ShapeDtypeStruct((T, D), F32),
        name="local_parts",
    )(queries, keys, values)


def project_kernel(
    q_ref, local_ref, prefix_ref, gain_ref, w_ref, res_ref, fgain_ref, sum_ref, normed_ref, att, acc
):
    step = pl.program_id(0)

    @pl.when(step == 0)
    def _():
        for h in range(HEADS):
            at = slice(h * DH, (h + 1) * DH)
            mixed = local_ref[:, at] + dot(q_ref[:, at], prefix_ref[h])
            scale = lax.rsqrt(jnp.mean(mixed * mixed, axis=-1, keepdims=True) + EPS)
            att[:, at] = (mixed * scale * gain_ref[:, at]).astype(BF)

    acc[step] = res_ref[...].astype(F32) + dot(att[...], w_ref[...])

    @pl.when(step == D // TILE - 1)
    def _():
        total = jnp.concatenate([acc[i] for i in range(D // TILE)], axis=1)
        norm = lax.rsqrt(jnp.mean(total * total, axis=-1, keepdims=True) + EPS)
        sum_ref[...] = total
        normed_ref[...] = (total * norm * fgain_ref[...]).astype(BF)


def project(queries, local, prefix_low, attn_gain, weight, residual, ffn_gain, after):
    after = [corner(v) if v.size > 1024 else v for v in after]
    whole = pl.BlockSpec((T, D), lambda j: (0, 0))
    row = pl.BlockSpec((1, D), lambda j: (0, 0))
    weight = pltpu.with_memory_space_constraint(weight, pltpu.HBM)
    return pl.pallas_call(
        untouched(project_kernel, len(after)),
        grid=(D // TILE,),
        in_specs=[UNREAD] * len(after)
        + [
            whole,
            whole,
            pl.BlockSpec((HEADS, DH, DH), lambda j: (0, 0, 0)),
            row,
            column_tile(D),
            column_tile(T),
            row,
        ],
        out_specs=[whole, whole],
        out_shape=[jax.ShapeDtypeStruct((T, D), F32), jax.ShapeDtypeStruct((T, D), BF)],
        scratch_shapes=[pltpu.VMEM((T, D), BF), pltpu.VMEM((D // TILE, T, TILE), F32)],
        compiler_params=pltpu.CompilerParams(vmem_limit_bytes=20 * MIB),
        name="project",
    )(*after, queries, local, prefix_low, attn_gain, weight, residual, ffn_gain)


def route_tables(meta, z, c):
    meta = jnp.stack([meta, shift(meta, "c", 1)])[None]
    for step in (1, 2, 4):
        meta = jnp.concatenate([meta, shift(meta, "z", -step)], axis=0)
    meta = jnp.concatenate([meta[k : k + 1] for chunk in CHUNKS for k in chunk], axis=0)
    meta = meta.reshape(2 * NZ, 8, T)
    picks, gains = meta[:, :MOST], meta[:, MOST:]
    offsets = jnp.arange(NX, dtype=jnp.int32)
    experts = ((2 * z + c) * NX + offsets).astype(F32)
    hit = picks[:, None, :, :] == experts[None, :, None, None]
    named = jnp.any(hit, axis=2)
    gain = jnp.sum(jnp.where(hit, gains[:, None], 0.0), axis=2)
    frame = jnp.arange(T, dtype=jnp.int32)
    earlier = (frame[:, None] < frame[None, :]) & (frame[:, None] // BLK == frame[None, :] // BLK)
    rank = lax.dot_general(
        named.astype(BF), earlier.astype(BF), (((2,), (0,)), ((), ())), preferred_element_type=F32
    )
    slot = rank.astype(jnp.int32) + frame // BLK * MOST
    taken = named & (rank < MOST)
    match = taken[:, :, None, :] & (
        slot[:, :, None, :] == jnp.arange(SLOTS, dtype=jnp.int32)[None, None, :, None]
    )
    select = match.astype(BF).reshape(2 * NZ, NX * SLOTS, T)
    high = lax.reduce_precision(gain, 8, 7)
    low = gain - high
    split = [
        jnp.where(match, part[:, :, None, :], 0.0).astype(BF).reshape(2 * NZ, NX * SLOTS, T)
        for part in (high, low)
    ]
    return select, jnp.concatenate(split, axis=1)


def pick_kernel(count, first, s_ref, *refs):
    out, token = refs[count:]
    token[...] = jnp.zeros_like(token)
    for i in range(count):
        rows = dot(s_ref[first + i], refs[i][...]).astype(BF)
        for j in range(NX):
            out[j, pl.ds(i * SLOTS, SLOTS), :] = rows[j * SLOTS : (j + 1) * SLOTS]


def pick_rows(select, first, blocks, after):
    count = len(blocks)
    after = [corner(v) if v.size > 1024 else v for v in after]
    return pl.pallas_call(
        untouched(lambda *refs: pick_kernel(count, first, *refs), len(after)),
        in_specs=[UNREAD] * len(after) + [ON_CHIP] * (1 + count),
        out_specs=[ON_CHIP] * 2,
        out_shape=[jax.ShapeDtypeStruct((NX, count * SLOTS, D), BF), TOKEN],
        name="pick_rows",
    )(*after, select, *blocks)


def mix_kernel(count, first, t_ref, rows_ref, own_ref, other_ref):
    for i in range(count):
        at = pl.ds(i * SLOTS, SLOTS)
        out = other_ref if i % 2 else own_ref
        for j in range(0, D, TILE):
            rows = jnp.concatenate([rows_ref[e, at, j : j + TILE] for e in range(NX)] * 2, axis=0)
            out[pl.ds(i // 2 * T, T), j : j + TILE] = dot(t_ref[first + i], rows, 0, 0).astype(BF)


def mix_rows(weights, first, rows, after):
    count = rows.shape[1] // SLOTS
    after = [corner(v) if v.size > 1024 else v for v in after]
    return pl.pallas_call(
        untouched(lambda *refs: mix_kernel(count, first, *refs), len(after)),
        in_specs=[UNREAD] * len(after) + [ON_CHIP] * 2,
        out_specs=[ON_CHIP] * 2,
        out_shape=[jax.ShapeDtypeStruct((count // 2 * T, D), BF)] * 2,
        name="mix_rows",
    )(*after, weights, rows)


def expert_kernel(sizes, at_y, *refs):
    n_in = len(sizes)
    inputs, weights = refs[:n_in], refs[n_in : n_in + 6]
    outs, token = refs[n_in + 6 : 2 * n_in + 6], refs[2 * n_in + 6]
    x_buf, g_buf, u_buf, d_buf, h_buf, o_buf, x_sem, g_sem, u_sem, d_sem, o_sem = refs[2 * n_in + 7 :]
    token[...] = jnp.zeros_like(token)
    starts = [sum(sizes[:i]) for i in range(n_in)]
    rows = sum(sizes)
    half = D // 2
    targets = [(0, 0, D), (1, 0, D), (2, 0, D), (3, 0, half), (3, half, half)]
    x_copies = [
        pltpu.make_async_copy(inputs[i], x_buf.at[pl.ds(starts[i], sizes[i])], x_sem.at[i])
        for i in range(n_in)
    ]
    g_copies = [
        pltpu.make_async_copy(weights[i], g_buf.at[g, pl.ds(first, size)], g_sem.at[i])
        for i, (g, first, size) in enumerate(targets)
    ]
    u_copies, d_copies = [], []
    for i, offset in enumerate((0, 3, 1, 2)):
        piece = weights[5].at[lax.rem(at_y[0] + offset, 4)]
        u_copies.append(pltpu.make_async_copy(piece.at[pl.ds(0, D)], u_buf.at[i], u_sem.at[i]))
        for j in range(D // HID):
            d_copies.append(
                pltpu.make_async_copy(
                    piece.at[pl.ds(D + j * HID, HID)],
                    d_buf.at[pl.ds(i * HID, HID), pl.ds(j * HID, HID)],
                    d_sem.at[i * (D // HID) + j],
                )
            )
    for copy in x_copies:
        copy.start()
    for i in range(4):
        g_copies[i].start()
        if i == 3:
            g_copies[4].start()
        u_copies[i].start()
    for copy in d_copies:
        copy.start()
    for copy in x_copies:
        copy.wait()
    for g in range(4):
        g_copies[g].wait()
        if g == 3:
            g_copies[4].wait()
        u_copies[g].wait()
        gate = dot(x_buf[...], g_buf[g])
        up = dot(x_buf[...], u_buf[g])
        h_buf[:, g * HID : (g + 1) * HID] = (gate / (1.0 + jnp.exp(-gate)) * up).astype(BF)
    for copy in d_copies:
        copy.wait()

    def out_columns(j, _):
        at = pl.ds(pl.multiple_of(j * TILE, TILE), TILE)
        o_buf[:, at] = dot(h_buf[...], d_buf[:, at]).astype(BF)
        return 0

    lax.fori_loop(0, D // TILE, out_columns, 0)
    o_copies = []
    for i in range(n_in):
        copy = pltpu.make_async_copy(o_buf.at[pl.ds(starts[i], sizes[i])], outs[i], o_sem.at[i])
        copy.start()
        o_copies.append(copy)
    for copy in o_copies:
        copy.wait()


def experts_apply(at_y, chunks, weights, after):
    after = [corner(v) if v.size > 1024 else v for v in after]
    buffers = [chunk.reshape(-1, D) for chunk in chunks]
    sizes = tuple(b.shape[0] for b in buffers)
    rows = sum(sizes)
    *outs, token = pl.pallas_call(
        untouched(lambda *refs: expert_kernel(sizes, *refs), len(after)),
        in_specs=[UNREAD] * len(after)
        + [pl.BlockSpec(memory_space=pltpu.SMEM)]
        + [ANYWHERE] * len(sizes)
        + [UNREAD] * 6,
        out_specs=[ANYWHERE] * len(sizes) + [ON_CHIP],
        out_shape=[jax.ShapeDtypeStruct((n, D), BF) for n in sizes] + [TOKEN],
        scratch_shapes=[
            pltpu.VMEM((rows, D), BF),
            pltpu.VMEM((4, D, HID), BF),
            pltpu.VMEM((4, D, HID), BF),
            pltpu.VMEM((4 * HID, D), BF),
            pltpu.VMEM((rows, 4 * HID), BF),
            pltpu.VMEM((rows, D), BF),
            pltpu.SemaphoreType.DMA((len(sizes),)),
            pltpu.SemaphoreType.DMA((5,)),
            pltpu.SemaphoreType.DMA((4,)),
            pltpu.SemaphoreType.DMA((4 * (D // HID),)),
            pltpu.SemaphoreType.DMA((len(sizes),)),
        ],
        compiler_params=pltpu.CompilerParams(vmem_limit_bytes=26 * MIB),
        name="experts",
    )(*after, at_y, *buffers, *weights)
    return [out.reshape(chunk.shape) for out, chunk in zip(outs, chunks)], token


def join_pieces(piece):
    half = piece.shape[0] // 2
    below, above = shift(piece, "y", 1), shift(piece, "y", -1)
    far_first = shift(below[:half], "y", 1)
    far_second = shift(above[half:], "y", -1)
    return [piece, below, above, far_first, far_second]


def ring_add(own, other, places, ring):
    half = T // 2
    up, down = (
        own[p * T : (p + 1) * T].astype(F32) + other[p * T : (p + 1) * T].astype(F32)
        for p in (places[0], places[-1])
    )
    if not ring:
        return up[:half].astype(BF), down[half:].astype(BF)
    first, second = (r.astype(F32) for r in lax.optimization_barrier(tuple(ring)))
    if first.shape[0] == half:
        first = jnp.concatenate([first, jnp.zeros_like(first)], axis=0)
        second = jnp.concatenate([jnp.zeros_like(second), second], axis=0)
    return (up + first).astype(BF), (down + second).astype(BF)


def final_sum(residual_sum, own, other, up, down, place):
    at = slice(place * T, (place + 1) * T)
    mixture = own[at].astype(F32) + other[at].astype(F32) + up.astype(F32) + down.astype(F32)
    return (residual_sum + mixture).astype(BF)


def shards(
    queries, keys, values, residual_in, attn_gain, out_proj, ffn_gain,
    w_gate, w_up, w_down, routes, gates,
):
    y, z, c = (lax.axis_index(name) for name in ("y", "z", "c"))
    queries, keys, values = queries[0], keys[0], values[0]
    weight = lax.all_gather(out_proj, ("z", "c"), axis=0, tiled=True)
    packed = [w_up[0]] + [w_down[0][:, j : j + HID] for j in range(0, D, HID)]
    packed = lax.all_gather(jnp.concatenate(packed, axis=0), "y", axis=0)
    gate_pieces = join_pieces(w_gate[0])
    states = block_states(keys, values)
    token = token_after([states])
    states = lax.all_to_all(states, ("x", "y"), 0, 0, tiled=True)
    prefix_low = block_prefixes(states, [])
    prefix_low = lax.all_to_all(prefix_low, ("x", "y"), 0, 0, tiled=True)
    meta = jnp.concatenate([routes[0].T.astype(F32), gates[0].T], axis=0)
    local = local_parts(queries, keys, values)
    select, weights = route_tables(held(meta, token), z, c)
    residual_sum, normed = project(
        queries, local, prefix_low, attn_gain[None], weight, residual_in[0], ffn_gain[None],
        [select, weights] + gate_pieces[1:3],
    )
    blocks = [normed] + [None] * (NZ - 1)
    arrived, tokens = [], []
    firsts = [2 * sum(len(chunk) for chunk in CHUNKS[:i]) for i in range(len(CHUNKS))]
    def step_z(near, up):
        blocks[near] = shift(up, "z", -1)
        blocks[NZ - near] = shift(blocks[(1 - near) % NZ], "z", 1)

    def pick(chunk, after):
        pairs = [b for k in CHUNKS[chunk] for b in (blocks[k], shift(blocks[k], "c", 1))]
        picked, token = pick_rows(select, firsts[chunk], pairs, after)
        tokens.append(token)
        arrived.append(lax.all_to_all(picked, "x", 0, 0, tiled=True))

    step_z(1, blocks[0])
    pick(0, [])
    step_z(2, blocks[1])
    blocks[2] = tied(blocks[2], tokens)
    step_z(3, blocks[2])
    pick(1, [tokens[0], blocks[3]] + gate_pieces[3:])
    blocks[4] = shift(blocks[3], "z", -1)
    pick(2, [tokens[1]])
    pieces = gate_pieces + [packed]
    pieces = [pltpu.with_memory_space_constraint(w, pltpu.HBM) for w in pieces]
    at_y = y[None].astype(jnp.int32)
    near, token = experts_apply(at_y, arrived[:2], pieces, tokens[2:])
    (far,), _ = experts_apply(at_y, arrived[2:], pieces, [token])
    returned = [None] * 3
    returned[1] = lax.all_to_all(tied(near[1], [corner(arrived[2])]), "x", 0, 0, tiled=True)
    returned[2] = lax.all_to_all(tied(far, [corner(returned[1])]), "x", 0, 0, tiled=True)
    returned[0] = lax.all_to_all(tied(near[0], [corner(returned[2])]), "x", 0, 0, tiled=True)
    own, other = {}, {}

    def mix(chunk, after):
        own[chunk], theirs = mix_rows(weights, firsts[chunk], returned[chunk], after)
        other[chunk] = shift(theirs, "c", 1)

    def pass_on(chunk, places, ring, last=None):
        up, down = ring_add(own[chunk], other[chunk], places, ring)
        if last is not None:
            mix(last, [up])
        return [shift(up, "z", 1), shift(down, "z", -1)]

    mix(1, [])
    mix(2, [own[1]])
    ring = pass_on(2, (1,), [])
    ring = pass_on(2, (0, 2), ring)
    ring = pass_on(1, (0, 1), ring, 0)
    ring = pass_on(0, (0, 2), ring)
    return final_sum(residual_sum, own[0], other[0], *ring, 1)[None]


def solution(mesh):
    shape = (NX, mesh.devices.shape[0] // NX, mesh.devices.shape[1] // 2, 2)
    grid = Mesh(mesh.devices.reshape(shape), ("x", "y", "z", "c"))
    tm, ep = ("x", "y"), ("z", "c")
    frames = P(ep, tm, None)
    pieces = P(ep + tm, None, None)
    placed = (frames, frames, frames, frames, P(), P(ep, None), P(), pieces, pieces, pieces, frames, frames)
    return jax.shard_map(
        shards, mesh=grid, in_specs=placed, out_specs=frames, check_vma=False
    )
```

```python
import jax
import jax.numpy as jnp
from jax import lax
from jax.experimental import pallas as pl
from jax.experimental.pallas import tpu as pltpu
from jax.sharding import Mesh
from jax.sharding import PartitionSpec as P

HEADS = 16
DH = 128
D = 2048
T = 128
BLK = 32
MOST = 4
NX = 4
NZ = 8
SLOTS = T // BLK * MOST
HID = 256
EPS = 1e-05
MIB = 1 << 20
CHUNKS = ((1, 0, 7), (2, 6), (3, 4, 5))
BF = jnp.bfloat16
F32 = jnp.float32


def dot(a, b, ca=1, cb=0):
    return lax.dot_general(a, b, (((ca,), (cb,)), ((), ())), preferred_element_type=F32)


def shift(value, axis, step):
    count = lax.axis_size(axis)
    return lax.ppermute(value, axis, [(i, (i + step) % count) for i in range(count)])


TILE = 512
ANYWHERE = pl.BlockSpec(memory_space=pl.ANY)
UNREAD = pl.BlockSpec(memory_space=pltpu.HBM)
ON_CHIP = pl.BlockSpec(memory_space=pltpu.VMEM)
TOKEN = jax.ShapeDtypeStruct((8, 128), F32)
TOKEN_SPEC = pl.BlockSpec((8, 128), lambda j: (0, 0))


def column_tile(rows):
    return pl.BlockSpec((rows, TILE), lambda j: (0, j))


def state_kernel(k_ref, v_ref, state_ref):
    for h in range(HEADS):
        at = slice(h * DH, (h + 1) * DH)
        state_ref[h] = dot(k_ref[:, at], v_ref[:, at], 0, 0)


def block_states(keys, values):
    return pl.pallas_call(
        state_kernel,
        out_shape=jax.ShapeDtypeStruct((HEADS, DH, DH), F32),
        name="block_states",
    )(keys, values)


def prefix_kernel(state_ref, out_ref):
    running = jnp.zeros((DH, DH), F32)
    for i in range(HEADS):
        out_ref[i] = running.astype(BF)
        running = running + state_ref[i]


def corner(value):
    return lax.slice(value, (0,) * value.ndim, (1,) * (value.ndim - 2) + (16, 128))


def untouched(kernel, count):
    return lambda *refs: kernel(*refs[count:])


def block_prefixes(states, after):
    after = [corner(v) if v.size > 1024 else v for v in after]
    return pl.pallas_call(
        untouched(prefix_kernel, len(after)),
        in_specs=[UNREAD] * len(after) + [pl.BlockSpec(memory_space=pltpu.VMEM)],
        out_shape=jax.ShapeDtypeStruct(states.shape, BF),
        name="block_prefixes",
    )(*after, states)


def token_kernel(*refs):
    refs[-1][...] = jnp.zeros_like(refs[-1])


def token_after(after):
    after = [corner(v) for v in after]
    return pl.pallas_call(
        token_kernel,
        in_specs=[UNREAD] * len(after),
        out_shape=TOKEN,
        name="token_after",
    )(*after)


def held(value, token):
    return jnp.where(token[0, 0] == 0.0, value, jnp.zeros_like(value))


def tied(value, after):
    after = [corner(v) if v.size > 1024 else v for v in after]
    return pl.pallas_call(
        lambda *refs: None,
        in_specs=[ANYWHERE] + [UNREAD] * len(after),
        out_specs=ANYWHERE,
        out_shape=jax.ShapeDtypeStruct(value.shape, value.dtype),
        input_output_aliases={0: 0},
        name="tied",
    )(value, *after)


def local_kernel(q_ref, k_ref, v_ref, out_ref):
    rows = lax.broadcasted_iota(jnp.int32, (T, T), 0)
    columns = lax.broadcasted_iota(jnp.int32, (T, T), 1)
    for h in range(4):
        at = slice(h * DH, (h + 1) * DH)
        scores = dot(q_ref[:, at], k_ref[:, at], 1, 1)
        scores = jnp.where(rows >= columns, scores, 0.0).astype(BF)
        out_ref[:, at] = dot(scores, v_ref[:, at])


def local_parts(queries, keys, values):
    heads = pl.BlockSpec((T, 4 * DH), lambda h: (0, h))
    return pl.pallas_call(
        local_kernel,
        grid=(HEADS // 4,),
        in_specs=[heads] * 3,
        out_specs=heads,
        out_shape=jax.ShapeDtypeStruct((T, D), F32),
        name="local_parts",
    )(queries, keys, values)


def project_kernel(
    q_ref, local_ref, prefix_ref, gain_ref, w_ref, res_ref, fgain_ref, sum_ref, normed_ref, att, acc
):
    step = pl.program_id(0)

    @pl.when(step == 0)
    def _():
        for h in range(HEADS):
            at = slice(h * DH, (h + 1) * DH)
            mixed = local_ref[:, at] + dot(q_ref[:, at], prefix_ref[h])
            scale = lax.rsqrt(jnp.mean(mixed * mixed, axis=-1, keepdims=True) + EPS)
            att[:, at] = (mixed * scale * gain_ref[:, at]).astype(BF)

    acc[step] = res_ref[...].astype(F32) + dot(att[...], w_ref[...])

    @pl.when(step == D // TILE - 1)
    def _():
        total = jnp.concatenate([acc[i] for i in range(D // TILE)], axis=1)
        norm = lax.rsqrt(jnp.mean(total * total, axis=-1, keepdims=True) + EPS)
        sum_ref[...] = total
        normed_ref[...] = (total * norm * fgain_ref[...]).astype(BF)


def project(queries, local, prefix_low, attn_gain, weight, residual, ffn_gain, after):
    after = [corner(v) if v.size > 1024 else v for v in after]
    whole = pl.BlockSpec((T, D), lambda j: (0, 0))
    row = pl.BlockSpec((1, D), lambda j: (0, 0))
    weight = pltpu.with_memory_space_constraint(weight, pltpu.HBM)
    return pl.pallas_call(
        untouched(project_kernel, len(after)),
        grid=(D // TILE,),
        in_specs=[UNREAD] * len(after)
        + [
            whole,
            whole,
            pl.BlockSpec((HEADS, DH, DH), lambda j: (0, 0, 0)),
            row,
            column_tile(D),
            column_tile(T),
            row,
        ],
        out_specs=[whole, whole],
        out_shape=[jax.ShapeDtypeStruct((T, D), F32), jax.ShapeDtypeStruct((T, D), BF)],
        scratch_shapes=[pltpu.VMEM((T, D), BF), pltpu.VMEM((D // TILE, T, TILE), F32)],
        compiler_params=pltpu.CompilerParams(vmem_limit_bytes=20 * MIB),
        name="project",
    )(*after, queries, local, prefix_low, attn_gain, weight, residual, ffn_gain)


def route_tables(meta, z, c):
    meta = jnp.stack([meta, shift(meta, "c", 1)])[None]
    for step in (1, 2, 4):
        meta = jnp.concatenate([meta, shift(meta, "z", -step)], axis=0)
    meta = jnp.concatenate([meta[k : k + 1] for chunk in CHUNKS for k in chunk], axis=0)
    meta = meta.reshape(2 * NZ, 8, T)
    picks, gains = meta[:, :MOST], meta[:, MOST:]
    offsets = jnp.arange(NX, dtype=jnp.int32)
    experts = ((2 * z + c) * NX + offsets).astype(F32)
    hit = picks[:, None, :, :] == experts[None, :, None, None]
    named = jnp.any(hit, axis=2)
    gain = jnp.sum(jnp.where(hit, gains[:, None], 0.0), axis=2)
    frame = jnp.arange(T, dtype=jnp.int32)
    earlier = (frame[:, None] < frame[None, :]) & (frame[:, None] // BLK == frame[None, :] // BLK)
    rank = lax.dot_general(
        named.astype(BF), earlier.astype(BF), (((2,), (0,)), ((), ())), preferred_element_type=F32
    )
    slot = rank.astype(jnp.int32) + frame // BLK * MOST
    taken = named & (rank < MOST)
    match = taken[:, :, None, :] & (
        slot[:, :, None, :] == jnp.arange(SLOTS, dtype=jnp.int32)[None, None, :, None]
    )
    select = match.astype(BF).reshape(2 * NZ, NX * SLOTS, T)
    high = lax.reduce_precision(gain, 8, 7)
    low = gain - high
    split = [
        jnp.where(match, part[:, :, None, :], 0.0).astype(BF).reshape(2 * NZ, NX * SLOTS, T)
        for part in (high, low)
    ]
    return select, jnp.concatenate(split, axis=1)


def pick_kernel(count, first, s_ref, *refs):
    out, token = refs[count:]
    token[...] = jnp.zeros_like(token)
    for i in range(count):
        rows = dot(s_ref[first + i], refs[i][...]).astype(BF)
        for j in range(NX):
            out[j, pl.ds(i * SLOTS, SLOTS), :] = rows[j * SLOTS : (j + 1) * SLOTS]


def pick_rows(select, first, blocks, after):
    count = len(blocks)
    after = [corner(v) if v.size > 1024 else v for v in after]
    return pl.pallas_call(
        untouched(lambda *refs: pick_kernel(count, first, *refs), len(after)),
        in_specs=[UNREAD] * len(after) + [ON_CHIP] * (1 + count),
        out_specs=[ON_CHIP] * 2,
        out_shape=[jax.ShapeDtypeStruct((NX, count * SLOTS, D), BF), TOKEN],
        name="pick_rows",
    )(*after, select, *blocks)


def mix_kernel(count, first, t_ref, rows_ref, own_ref, other_ref):
    for i in range(count):
        at = pl.ds(i * SLOTS, SLOTS)
        out = other_ref if i % 2 else own_ref
        for j in range(0, D, TILE):
            rows = jnp.concatenate([rows_ref[e, at, j : j + TILE] for e in range(NX)] * 2, axis=0)
            out[pl.ds(i // 2 * T, T), j : j + TILE] = dot(t_ref[first + i], rows, 0, 0).astype(BF)


def mix_rows(weights, first, rows, after):
    count = rows.shape[1] // SLOTS
    after = [corner(v) if v.size > 1024 else v for v in after]
    return pl.pallas_call(
        untouched(lambda *refs: mix_kernel(count, first, *refs), len(after)),
        in_specs=[UNREAD] * len(after) + [ON_CHIP] * 2,
        out_specs=[ON_CHIP] * 2,
        out_shape=[jax.ShapeDtypeStruct((count // 2 * T, D), BF)] * 2,
        name="mix_rows",
    )(*after, weights, rows)


def expert_kernel(sizes, at_y, *refs):
    n_in = len(sizes)
    inputs, weights = refs[:n_in], refs[n_in : n_in + 6]
    outs, token = refs[n_in + 6 : 2 * n_in + 6], refs[2 * n_in + 6]
    x_buf, g_buf, u_buf, d_buf, h_buf, o_buf, x_sem, g_sem, u_sem, d_sem, o_sem = refs[2 * n_in + 7 :]
    token[...] = jnp.zeros_like(token)
    starts = [sum(sizes[:i]) for i in range(n_in)]
    rows = sum(sizes)
    half = D // 2
    targets = [(0, 0, D), (1, 0, D), (2, 0, D), (3, 0, half), (3, half, half)]
    x_copies = [
        pltpu.make_async_copy(inputs[i], x_buf.at[pl.ds(starts[i], sizes[i])], x_sem.at[i])
        for i in range(n_in)
    ]
    g_copies = [
        pltpu.make_async_copy(weights[i], g_buf.at[g, pl.ds(first, size)], g_sem.at[i])
        for i, (g, first, size) in enumerate(targets)
    ]
    u_copies, d_copies = [], []
    for i, offset in enumerate((0, 3, 1, 2)):
        piece = weights[5].at[lax.rem(at_y[0] + offset, 4)]
        u_copies.append(pltpu.make_async_copy(piece.at[pl.ds(0, D)], u_buf.at[i], u_sem.at[i]))
        for j in range(D // HID):
            d_copies.append(
                pltpu.make_async_copy(
                    piece.at[pl.ds(D + j * HID, HID)],
                    d_buf.at[pl.ds(i * HID, HID), pl.ds(j * HID, HID)],
                    d_sem.at[i * (D // HID) + j],
                )
            )
    for copy in x_copies:
        copy.start()
    for i in range(4):
        g_copies[i].start()
        if i == 3:
            g_copies[4].start()
        u_copies[i].start()
    for copy in d_copies:
        copy.start()
    for copy in x_copies:
        copy.wait()
    for g in range(4):
        g_copies[g].wait()
        if g == 3:
            g_copies[4].wait()
        u_copies[g].wait()
        gate = dot(x_buf[...], g_buf[g])
        up = dot(x_buf[...], u_buf[g])
        h_buf[:, g * HID : (g + 1) * HID] = (gate / (1.0 + jnp.exp(-gate)) * up).astype(BF)
    for copy in d_copies:
        copy.wait()

    def out_columns(j, _):
        at = pl.ds(pl.multiple_of(j * TILE, TILE), TILE)
        o_buf[:, at] = dot(h_buf[...], d_buf[:, at]).astype(BF)
        return 0

    lax.fori_loop(0, D // TILE, out_columns, 0)
    o_copies = []
    for i in range(n_in):
        copy = pltpu.make_async_copy(o_buf.at[pl.ds(starts[i], sizes[i])], outs[i], o_sem.at[i])
        copy.start()
        o_copies.append(copy)
    for copy in o_copies:
        copy.wait()


def experts_apply(at_y, chunks, weights, after):
    after = [corner(v) if v.size > 1024 else v for v in after]
    buffers = [chunk.reshape(-1, D) for chunk in chunks]
    sizes = tuple(b.shape[0] for b in buffers)
    rows = sum(sizes)
    *outs, token = pl.pallas_call(
        untouched(lambda *refs: expert_kernel(sizes, *refs), len(after)),
        in_specs=[UNREAD] * len(after)
        + [pl.BlockSpec(memory_space=pltpu.SMEM)]
        + [ANYWHERE] * len(sizes)
        + [UNREAD] * 6,
        out_specs=[ANYWHERE] * len(sizes) + [ON_CHIP],
        out_shape=[jax.ShapeDtypeStruct((n, D), BF) for n in sizes] + [TOKEN],
        scratch_shapes=[
            pltpu.VMEM((rows, D), BF),
            pltpu.VMEM((4, D, HID), BF),
            pltpu.VMEM((4, D, HID), BF),
            pltpu.VMEM((4 * HID, D), BF),
            pltpu.VMEM((rows, 4 * HID), BF),
            pltpu.VMEM((rows, D), BF),
            pltpu.SemaphoreType.DMA((len(sizes),)),
            pltpu.SemaphoreType.DMA((5,)),
            pltpu.SemaphoreType.DMA((4,)),
            pltpu.SemaphoreType.DMA((4 * (D // HID),)),
            pltpu.SemaphoreType.DMA((len(sizes),)),
        ],
        compiler_params=pltpu.CompilerParams(vmem_limit_bytes=26 * MIB),
        name="experts",
    )(*after, at_y, *buffers, *weights)
    return [out.reshape(chunk.shape) for out, chunk in zip(outs, chunks)], token


def join_pieces(piece):
    half = piece.shape[0] // 2
    below, above = shift(piece, "y", 1), shift(piece, "y", -1)
    far_first = shift(below[:half], "y", 1)
    far_second = shift(above[half:], "y", -1)
    return [piece, below, above, far_first, far_second]


def ring_add(own, other, places, ring):
    half = T // 2
    up, down = (
        own[p * T : (p + 1) * T].astype(F32) + other[p * T : (p + 1) * T].astype(F32)
        for p in (places[0], places[-1])
    )
    if not ring:
        return up[:half].astype(BF), down[half:].astype(BF)
    first, second = (r.astype(F32) for r in lax.optimization_barrier(tuple(ring)))
    if first.shape[0] == half:
        first = jnp.concatenate([first, jnp.zeros_like(first)], axis=0)
        second = jnp.concatenate([jnp.zeros_like(second), second], axis=0)
    return (up + first).astype(BF), (down + second).astype(BF)


def final_sum(residual_sum, own, other, up, down, place):
    at = slice(place * T, (place + 1) * T)
    mixture = own[at].astype(F32) + other[at].astype(F32) + up.astype(F32) + down.astype(F32)
    return (residual_sum + mixture).astype(BF)


def shards(
    queries, keys, values, residual_in, attn_gain, out_proj, ffn_gain,
    w_gate, w_up, w_down, routes, gates,
):
    y, z, c = (lax.axis_index(name) for name in ("y", "z", "c"))
    queries, keys, values = queries[0], keys[0], values[0]
    weight = lax.all_gather(out_proj, ("z", "c"), axis=0, tiled=True)
    packed = [w_up[0]] + [w_down[0][:, j : j + HID] for j in range(0, D, HID)]
    packed = lax.all_gather(jnp.concatenate(packed, axis=0), "y", axis=0)
    gate_pieces = join_pieces(w_gate[0])
    states = block_states(keys, values)
    token = token_after([states])
    states = lax.all_to_all(states, ("x", "y"), 0, 0, tiled=True)
    prefix_low = block_prefixes(states, [])
    prefix_low = lax.all_to_all(prefix_low, ("x", "y"), 0, 0, tiled=True)
    meta = jnp.concatenate([routes[0].T.astype(F32), gates[0].T], axis=0)
    local = local_parts(queries, keys, values)
    select, weights = route_tables(held(meta, token), z, c)
    residual_sum, normed = project(
        queries, local, prefix_low, attn_gain[None], weight, residual_in[0], ffn_gain[None],
        [select, weights] + gate_pieces[1:3],
    )
    blocks = [normed] + [None] * (NZ - 1)
    arrived, tokens = [], []
    firsts = [2 * sum(len(chunk) for chunk in CHUNKS[:i]) for i in range(len(CHUNKS))]
    def step_z(near, up):
        blocks[near] = shift(up, "z", -1)
        blocks[NZ - near] = shift(blocks[(1 - near) % NZ], "z", 1)

    def pick(chunk, after):
        pairs = [b for k in CHUNKS[chunk] for b in (blocks[k], shift(blocks[k], "c", 1))]
        picked, token = pick_rows(select, firsts[chunk], pairs, after)
        tokens.append(token)
        arrived.append(lax.all_to_all(picked, "x", 0, 0, tiled=True))

    step_z(1, blocks[0])
    pick(0, [])
    step_z(2, blocks[1])
    blocks[2] = tied(blocks[2], tokens)
    step_z(3, blocks[2])
    pick(1, [tokens[0], blocks[3]])
    blocks[4] = shift(blocks[3], "z", -1)
    pick(2, [tokens[1]] + gate_pieces[3:])
    pieces = gate_pieces + [packed]
    pieces = [pltpu.with_memory_space_constraint(w, pltpu.HBM) for w in pieces]
    at_y = y[None].astype(jnp.int32)
    near, token = experts_apply(at_y, arrived[:2], pieces, tokens[2:])
    (far,), _ = experts_apply(at_y, arrived[2:], pieces, [token])
    returned = [None] * 3
    returned[1] = lax.all_to_all(tied(near[1], [corner(arrived[2])]), "x", 0, 0, tiled=True)
    returned[2] = lax.all_to_all(tied(far, [corner(returned[1])]), "x", 0, 0, tiled=True)
    returned[0] = lax.all_to_all(tied(near[0], [corner(returned[2])]), "x", 0, 0, tiled=True)
    own, other = {}, {}

    def mix(chunk, after):
        own[chunk], theirs = mix_rows(weights, firsts[chunk], returned[chunk], after)
        other[chunk] = shift(theirs, "c", 1)

    def pass_on(chunk, places, ring, last=None):
        up, down = ring_add(own[chunk], other[chunk], places, ring)
        if last is not None:
            mix(last, [up])
        return [shift(up, "z", 1), shift(down, "z", -1)]

    mix(1, [])
    mix(2, [own[1]])
    ring = pass_on(2, (1,), [])
    ring = pass_on(2, (0, 2), ring)
    ring = pass_on(1, (0, 1), ring, 0)
    ring = pass_on(0, (0, 2), ring)
    return final_sum(residual_sum, own[0], other[0], *ring, 1)[None]


def solution(mesh):
    shape = (NX, mesh.devices.shape[0] // NX, mesh.devices.shape[1] // 2, 2)
    grid = Mesh(mesh.devices.reshape(shape), ("x", "y", "z", "c"))
    tm, ep = ("x", "y"), ("z", "c")
    frames = P(ep, tm, None)
    pieces = P(ep + tm, None, None)
    placed = (frames, frames, frames, frames, P(), P(ep, None), P(), pieces, pieces, pieces, frames, frames)
    return jax.shard_map(
        shards, mesh=grid, in_specs=placed, out_specs=frames, check_vma=False
    )
```
